256 devices in a mesh: dp: 32 (over x, z), chan: 8 (over y, core).
Axes of the slice: x: 4, y: 4, z: 8, core: 2. Of those that a mesh axis runs over, the one named last changes fastest.
Arguments:
- latents: bfloat16 [1024, 4, 8, 640], P('dp', None, 'chan'), may hold values from -6 to 6
- bucket_ids: int32 [1024, 1], P('dp'), may hold values from 0 to 31; in each aligned block of 32 rows (0 to 31, 32 to 63, ...) at most 2 rows name the same one
- timesteps: int32 [1024], P('dp'), may hold values from 0 to 999
- time_table: bfloat16 [250, 8, 640], P(None, 'chan'), may hold values from -6 to 6
- norm_gain: float32 [1280], P('chan'), may hold values from 0.25 to 1.75
- norm_bias: float32 [1280], P('chan'), may hold values from -3 to 3
- conv_weight: bfloat16 [3, 3, 1280, 1280], P(None, None, 'chan'), may hold values from -0.0546875 to 0.0546875
- cotangent: bfloat16 [2048, 4, 8, 640], P('dp', None, 'chan'), may hold values from -6 to 6
Outputs:
- out_slots: bfloat16 [2048, 4, 8, 640], P('dp', None, 'chan')
- grad_slots: bfloat16 [2048, 4, 8, 640], P('dp', None, 'chan')
- grad_weight: float32 [3, 3, 1280, 1280], P(None, None, 'chan')
- grad_norm: float32 [2, 1280], P(None, 'chan')
The draws below stay inside these ranges and needn't reach their ends.
Inputs may be any that keep to these rules, and one draw needn't show every extreme that they name: `bucket_ids`: bucket b belongs to index b of dp. Among the samples of one dp index at most 2 name the same bucket, and exactly 2 do for some bucket.
All inputs are finite; a program needn't handle non-finite values.
Results may differ from the reference program's by a relative error of at most 0.0029.
Values may be sent and summed in bfloat16 or wider, within the bound.
No kernel may reach another device: no remote copies, remote signals or barrier semaphores. Data moves between devices by JAX's collectives and lax.ppermute only.
A program may use at most 192 MiB of HBM per device.

```python
import math
import jax
import jax.numpy as jnp
import numpy as np
from jax import lax

C = 1280
GROUPS = 32
STEPS = 1000
H = 4
W = 4
SAMP_DEV = 32
CB = 160
CAP = 2
LIVE = 1024
SLOTS = 2048
N_DP = 32
N_CHAN = 8


def set_ends(result, stream_key, low, high):
    longest = result.shape.index(max(result.shape))
    spots = []
    for shift in (0, 1):
        where = [jax.random.randint(jax.random.fold_in(stream_key, axis), (), 0, length) for axis, length in enumerate(result.shape)]
        where[longest] = (where[longest] + shift) % result.shape[longest]
        spots.append(tuple(where))
    return result.at[spots[0]].set(low).at[spots[1]].set(high)


def shard_levels(own_key, shape, cuts, low, high):
    factor_of, own = 1.0, jax.random.fold_in(own_key, 6)
    for dim, shards_of in cuts:
        heights = jnp.exp(jax.random.uniform(jax.random.fold_in(own, dim), (shards_of,), jnp.float32, low / len(cuts), high / len(cuts)))
        factor_of = factor_of * jnp.repeat(heights, shape[dim] // shards_of).reshape([-1 if axis == dim else 1 for axis in range(len(shape))])
    return factor_of


def shared_out(rng, own, number, rows, count, top, bound, skew):
    order = jax.random.permutation(rng, count)
    heavy_load, ordinary = load_shares(count, rows * top, bound, skew, True), load_shares(count, rows * top, bound, skew, False)
    places = jnp.arange(count)

    def named(tallies, rotation):
        used = int((tallies > 0).sum())
        fixed = max(1, used // 4)
        passed = fixed + (places - fixed + rotation * (used - fixed)) % max(1, count - fixed)
        return jnp.zeros((count,), jnp.int32).at[order[jnp.where(places < fixed, places, passed)]].set(jnp.asarray(tallies, jnp.int32))

    tallies = jnp.where(number % 4 == 0, named(heavy_load, number // 4), named(ordinary, number - number // 4 - 1))
    mixed = jax.random.permutation(jax.random.fold_in(own, 3), count)
    giver, taker = mixed[0:count // 2 * 2:2], mixed[1:count // 2 * 2:2]
    room = jnp.minimum(tallies[giver] - 1, bound - tallies[taker]) // 2
    room = jnp.where((giver == order[0]) | (taker == order[0]) | (tallies[taker] == 0), 0, jnp.maximum(room, 0))
    passed = jax.random.randint(jax.random.fold_in(own, 4), (count // 2,), 0, 1 << 20) % (room + 1)
    tallies = tallies.at[giver].add(-passed).at[taker].add(passed)
    items = jnp.searchsorted(jnp.cumsum(tallies), jnp.arange(rows * top), side="right").astype(jnp.int32)
    grid = items.reshape(top, rows).T
    grid = grid[jax.random.permutation(jax.random.fold_in(own, 1), rows)]
    rotation = jax.random.randint(jax.random.fold_in(own, 2), (rows, 1), 0, top)
    return jnp.take_along_axis(grid, (jnp.arange(top)[None, :] + rotation) % top, axis=1)


def load_shares(amount, total, most, slope, full):
    weights = [(1 << 20) // math.isqrt(standing ** slope) + 1 for standing in range(1, amount + 1)]
    largest = most if full else min(most, max(-(-total // amount), total * weights[0] // sum(weights)))
    least = 1 if total - largest >= amount - 1 else 0
    counts, surplus = [largest] + [least] * (amount - 1), total - largest - least * (amount - 1)
    while surplus > 0:
        free = [i for i in range(1, amount) if counts[i] < largest] or [i for i in range(1, amount) if counts[i] < most]
        mass, budget = sum([weights[i] for i in free]), surplus
        for i in free:
            more = min(most - counts[i], max(1, budget * weights[i] // mass), surplus)
            counts[i] = counts[i] + more
            surplus = surplus - more
    return np.array(counts)


def scatter_about(own_key, dims, spread, limit, shards=(), kind=jnp.bfloat16):
    result = spread * jax.random.normal(own_key, dims, jnp.float32)
    if shards:
        result = result * shard_levels(own_key, dims, shards, -0.22, 0.18)
    return jnp.clip(result, -limit, limit).astype(kind)


def setup_inputs(seed: int = 0) -> dict:
    key_of = jax.random.split(jax.random.key(seed), 9)
    latents = scatter_about(key_of[0], (LIVE, H, N_CHAN, W * CB), 1.0, 6.0, ((0, 32), (2, 8)))
    bucket_ids_keys = jax.random.split(jax.random.fold_in(key_of[1], 1), LIVE // SAMP_DEV)
    bucket_ids_turns = jax.random.permutation(jax.random.fold_in(key_of[1], 3), LIVE // SAMP_DEV)
    bucket_ids = jax.vmap(lambda own, number: shared_out(jax.random.fold_in(key_of[1], 2), own, number, SAMP_DEV, N_DP, 1, CAP, 2))(bucket_ids_keys, bucket_ids_turns).reshape((LIVE, 1))
    timesteps = set_ends(jax.random.randint(key_of[2], (LIVE,), 0, STEPS), jax.random.fold_in(key_of[2], 1), 0, STEPS - 1).astype(jnp.int32)
    time_table = scatter_about(key_of[3], (STEPS // 4, N_CHAN, 4 * CB), 1.0, 6.0, ((1, 8),))
    norm_gain = jnp.clip(1.0 + 0.15 * jax.random.normal(key_of[4], (C,), jnp.float32), 0.25, 1.75)
    norm_bias = scatter_about(key_of[5], (C,), 0.5, 3.0, ((0, 8),), jnp.float32)
    conv_weight = scatter_about(key_of[6], (3, 3, C, C), (9 * C) ** -0.5, 0.0546875, ((2, 8),))
    cotangent = scatter_about(key_of[7], (SLOTS, H, N_CHAN, W * CB), 1.0, 6.0, ((0, 32), (2, 8)))
    return dict(latents=latents, bucket_ids=bucket_ids, timesteps=timesteps, time_table=time_table, norm_gain=norm_gain, norm_bias=norm_bias, conv_weight=conv_weight, cotangent=cotangent)


EPS = 1e-05

def to_maps(packed):
    count = packed.shape[0]
    blocks = packed.reshape(count, H, N_CHAN, W, C // N_CHAN)
    return jnp.transpose(blocks, (0, 1, 3, 2, 4)).reshape(count, H, W, C)

def from_maps(maps):
    count = maps.shape[0]
    blocks = maps.reshape(count, H, W, N_CHAN, C // N_CHAN)
    return jnp.transpose(blocks, (0, 1, 3, 2, 4)).reshape(count, H, N_CHAN, W * (C // N_CHAN))

def norm_forward(latents, gain, bias):
    count, height, breadth, chans_all = latents.shape
    group_size = C // GROUPS
    grouped = latents.astype(jnp.float32).reshape(count, height, breadth, chans_all // group_size, group_size)
    center = grouped - lax.optimization_barrier(jnp.mean(grouped, axis=(1, 2, 4), keepdims=True))
    inverse = lax.rsqrt(lax.optimization_barrier(jnp.mean(center * center, axis=(1, 2, 4), keepdims=True)) + EPS)
    normed = (center * inverse).reshape(count, height, breadth, chans_all)
    shifted = normed * gain + bias
    gate = jax.nn.sigmoid(shifted)
    activated = (shifted * gate).astype(jnp.bfloat16)
    return (normed, inverse, shifted, gate, activated)

def norm_backward(dact, normed, inverse, shifted, gate, gain):
    count, height, breadth, chans_all = normed.shape
    group_size = C // GROUPS
    dshift = dact * gate * (1.0 + shifted * (1.0 - gate))
    grad_gain = lax.optimization_barrier(jnp.sum(dshift * normed, axis=(0, 1, 2)))
    grad_bias = lax.optimization_barrier(jnp.sum(dshift, axis=(0, 1, 2)))
    dnormed = (dshift * gain).reshape(count, height, breadth, chans_all // group_size, group_size)
    grouped = normed.reshape(dnormed.shape)
    first = lax.optimization_barrier(jnp.mean(dnormed, axis=(1, 2, 4), keepdims=True))
    second = lax.optimization_barrier(jnp.mean(dnormed * grouped, axis=(1, 2, 4), keepdims=True))
    dinput = (inverse * (dnormed - first - grouped * second)).reshape(count, height, breadth, chans_all)
    return (dinput, grad_gain, grad_bias)

def reference(latents, bucket_ids, timesteps, time_table, norm_gain, norm_bias, conv_weight, cotangent):
    high = lax.Precision.HIGHEST
    maps_in = to_maps(latents)
    cot_maps = to_maps(cotangent)
    table = jnp.transpose(time_table.reshape(STEPS // 4, N_CHAN, 4, C // N_CHAN), (0, 2, 1, 3)).reshape(STEPS, C)
    buckets = bucket_ids[:, 0].reshape(N_DP, SAMP_DEV)
    onehot = (buckets[:, :, None] == jnp.arange(N_DP, dtype=jnp.int32)[None, None, :]).astype(jnp.int32)
    rank = lax.optimization_barrier(jnp.sum((jnp.cumsum(onehot, axis=1) - 1) * onehot, axis=2))
    source = jnp.arange(N_DP, dtype=jnp.int32)[:, None]
    rows = (buckets * (N_DP * CAP) + source * CAP + rank).reshape(-1).astype(jnp.int32)
    embed = table[timesteps].astype(jnp.float32)
    normed, inverse, shifted, gate, activated = norm_forward(maps_in, norm_gain, norm_bias)
    padded = jnp.pad(activated.astype(jnp.float32), ((0, 0), (1, 1), (1, 1), (0, 0)))
    weights = conv_weight.astype(jnp.float32)
    dout = cot_maps[rows].astype(jnp.float32)
    conv = jnp.zeros((LIVE, H, W, C), jnp.float32)
    grads = []
    dpad = jnp.zeros((LIVE, H + 2, W + 2, C), jnp.float32)
    for row_tap in range(3):
        for col_tap in range(3):
            tap = padded[:, row_tap:row_tap + H, col_tap:col_tap + W, :]
            conv = conv + jnp.einsum('shwi,oi->shwo', tap, weights[row_tap, col_tap], precision=high)
            grads.append(jnp.einsum('shwi,shwo->oi', tap, dout, precision=high))
            contrib = jnp.einsum('shwo,oi->shwi', dout, weights[row_tap, col_tap], precision=high)
            dpad = dpad.at[:, row_tap:row_tap + H, col_tap:col_tap + W, :].add(contrib)
    output = (maps_in.astype(jnp.float32) + conv + embed[:, None, None, :]).astype(jnp.bfloat16)
    dact = dpad[:, 1:-1, 1:-1, :]
    dinput, grad_gain, grad_bias = norm_backward(dact, normed, inverse, shifted, gate, norm_gain)
    grad_input = (dout + dinput).astype(jnp.bfloat16)
    scale = lax.rsqrt(jnp.float32(LIVE * H * W))
    out_maps = jnp.zeros((SLOTS, H, W, C), jnp.bfloat16).at[rows].set(output)
    grad_maps = jnp.zeros((SLOTS, H, W, C), jnp.bfloat16).at[rows].set(grad_input)
    grad_weight = jnp.stack(grads).reshape(3, 3, C, C) * scale
    grad_norm = jnp.stack([grad_gain, grad_bias]) * scale
    return (from_maps(out_maps), from_maps(grad_maps), grad_weight, grad_norm)
```

```python
import math

import jax
import jax.numpy as jnp
from jax import lax
from jax.sharding import PartitionSpec as P

C = 1280
GROUPS = 32
W = 4


EPS = 1e-05


def norm_forward(latents, gain, bias):
    count, height, breadth, local_chan = latents.shape
    group_size = C // GROUPS
    grouped = latents.astype(jnp.float32).reshape(
        count, height, breadth, local_chan // group_size, group_size
    )
    center = grouped - jnp.mean(grouped, axis=(1, 2, 4), keepdims=True)
    inverse = lax.rsqrt(jnp.mean(center * center, axis=(1, 2, 4), keepdims=True) + EPS)
    normed = (center * inverse).reshape(count, height, breadth, local_chan)
    shifted = normed * gain + bias
    gate = jax.nn.sigmoid(shifted)
    activated = (shifted * gate).astype(jnp.bfloat16)
    return (normed, inverse, shifted, gate, activated)


def norm_backward(dact, normed, inverse, shifted, gate, gain):
    count, height, breadth, local_chan = normed.shape
    group_size = C // GROUPS
    dshift = dact * gate * (1.0 + shifted * (1.0 - gate))
    grad_gain = jnp.sum(dshift * normed, axis=(0, 1, 2))
    grad_bias = jnp.sum(dshift, axis=(0, 1, 2))
    dnormed = (dshift * gain).reshape(count, height, breadth, local_chan // group_size, group_size)
    grouped = normed.reshape(dnormed.shape)
    first = jnp.mean(dnormed, axis=(1, 2, 4), keepdims=True)
    second = jnp.mean(dnormed * grouped, axis=(1, 2, 4), keepdims=True)
    dinput = (inverse * (dnormed - first - grouped * second)).reshape(
        count, height, breadth, local_chan
    )
    return (dinput, grad_gain, grad_bias)


def transpose_conv(grad_maps, weights):
    count, height, breadth, out_chan = grad_maps.shape
    in_chan = weights.shape[3]
    flat = grad_maps.reshape(-1, out_chan)
    total = jnp.zeros((count, height + 2, breadth + 2, in_chan), jnp.float32)
    for row_tap in range(3):
        for col_tap in range(3):
            contrib = jnp.dot(flat, weights[row_tap, col_tap], preferred_element_type=jnp.float32)
            contrib = contrib.reshape(count, height, breadth, in_chan)
            total = total + jnp.pad(
                contrib, ((0, 0), (row_tap, 2 - row_tap), (col_tap, 2 - col_tap), (0, 0))
            )
    return total[:, 1:-1, 1:-1, :]


def process(latents, embed, present, cotangent, gain, bias, weight):
    count, height, breadth, local_chan = latents.shape
    normed, inverse, shifted, gate, activated = norm_forward(latents, gain, bias)
    dout = (cotangent.astype(jnp.float32) * present[:, None, None, None]).astype(jnp.bfloat16)
    dout_flat = dout.reshape(-1, local_chan)
    start_conv = jnp.zeros((count, height, breadth, local_chan), jnp.float32)
    piece = lax.all_gather(activated, "chan", axis=3, tiled=True)
    conv = start_conv
    width_in = piece.shape[3]
    padded = jnp.pad(piece, ((0, 0), (1, 1), (1, 1), (0, 0)))
    blocks = []
    for row_tap in range(3):
        for col_tap in range(3):
            tap = padded[:, row_tap : row_tap + height, col_tap : col_tap + breadth, :].reshape(
                -1, width_in
            )
            term = lax.dot_general(
                tap,
                weight[row_tap, col_tap],
                (((1,), (1,)), ((), ())),
                preferred_element_type=jnp.float32,
            )
            conv = conv + term.reshape(conv.shape)
            blocks.append(jnp.dot(dout_flat.T, tap, preferred_element_type=jnp.float32))
    block = jnp.stack(blocks).reshape(3, 3, local_chan, width_in)
    grad_weight = block
    conv, grad_weight = (conv, grad_weight)
    partial_sums = transpose_conv(dout, weight)
    dact = lax.psum_scatter(partial_sums, "chan", scatter_dimension=3, tiled=True)
    dinput, grad_gain, grad_bias = norm_backward(dact, normed, inverse, shifted, gate, gain)
    grad_input = (dout.astype(jnp.float32) + dinput).astype(jnp.bfloat16)
    output = latents.astype(jnp.float32) + conv + embed.astype(jnp.float32)[:, None, None, :]
    output = (output * present[:, None, None, None]).astype(jnp.bfloat16)
    return (output, grad_input, (grad_weight, grad_gain, grad_bias))


def per_device(
    latents, bucket_ids, timesteps, time_table, norm_gain, norm_bias, conv_weight, cotangent
):
    dp_count = lax.axis_size("dp")
    samples = latents.shape[0]
    height = latents.shape[1]
    breadth = W
    local_chan = latents.shape[3] // breadth
    packed_last = latents.shape[3]
    maps_in = latents.reshape(samples, height, breadth, local_chan)
    slots_here = cotangent.shape[0]
    cot_maps = cotangent.reshape(slots_here, height, breadth, local_chan)
    capacity = slots_here // dp_count
    buckets = bucket_ids[:, 0]
    order = jnp.arange(samples, dtype=jnp.int32)
    earlier = (buckets[:, None] == buckets[None, :]) & (order[None, :] < order[:, None])
    rank = jnp.sum(earlier.astype(jnp.int32), axis=1)
    target = buckets * capacity + rank
    placing = (target[None, :] == jnp.arange(slots_here, dtype=jnp.int32)[:, None]).astype(
        jnp.bfloat16
    )
    table = time_table.reshape(-1, local_chan)
    steps_all = table.shape[0]
    picker = (timesteps[:, None] == jnp.arange(steps_all, dtype=jnp.int32)[None, :]).astype(
        jnp.bfloat16
    )
    embed = jnp.dot(picker, table, preferred_element_type=jnp.float32).astype(jnp.bfloat16)
    scale = 1.0 / math.sqrt(samples * dp_count * height * breadth)
    flat = maps_in.reshape(samples, -1)
    send_maps = jnp.dot(placing, flat, preferred_element_type=jnp.float32).astype(jnp.bfloat16)
    send_maps = send_maps.reshape(dp_count, capacity, height, breadth, local_chan)
    send_embed = jnp.dot(placing, embed, preferred_element_type=jnp.float32).astype(jnp.bfloat16)
    send_embed = send_embed.reshape(dp_count, capacity, local_chan)
    send_present = (
        jnp.sum(placing.astype(jnp.float32), axis=1)
        .astype(jnp.bfloat16)
        .reshape(dp_count, capacity)
    )
    got_maps, got_embed, got_present = (
        lax.all_to_all(send_maps, "dp", split_axis=0, concat_axis=0, tiled=True),
        lax.all_to_all(send_embed, "dp", split_axis=0, concat_axis=0, tiled=True),
        lax.all_to_all(send_present, "dp", split_axis=0, concat_axis=0, tiled=True),
    )
    got_maps = got_maps.reshape(slots_here, height, breadth, local_chan)
    got_embed = got_embed.reshape(slots_here, local_chan)
    got_present = got_present.reshape(slots_here).astype(jnp.float32)
    out_maps, grad_maps, sums = process(
        got_maps, got_embed, got_present, cot_maps, norm_gain, norm_bias, conv_weight
    )
    out_slots = out_maps.reshape(slots_here, height, 1, packed_last)
    grad_slots = grad_maps.reshape(slots_here, height, 1, packed_last)
    grad_weight, grad_gain, grad_bias = lax.psum((sums[0], sums[1], sums[2]), "dp")
    return (out_slots, grad_slots, grad_weight * scale, jnp.stack([grad_gain, grad_bias]) * scale)


def solution(mesh):
    in_specs = (
        P("dp", None, "chan", None),
        P("dp", None),
        P("dp"),
        P(None, "chan", None),
        P("chan"),
        P("chan"),
        P(None, None, "chan", None),
        P("dp", None, "chan", None),
    )
    out_specs = (
        P("dp", None, "chan", None),
        P("dp", None, "chan", None),
        P(None, None, "chan", None),
        P(None, "chan"),
    )
    return jax.shard_map(
        per_device, mesh=mesh, in_specs=in_specs, out_specs=out_specs, check_vma=False
    )
```

```python
import functools
import math

import jax
import jax.numpy as jnp
from jax import lax
from jax.experimental import pallas as pl
from jax.experimental.pallas import tpu as pltpu
from jax.sharding import PartitionSpec as P

C = 1280
GROUPS = 32
SIDE = 4
CELLS = 16
EPS = 1e-05
NX = 4
NZ = 8
F32 = jnp.float32
BF16 = jnp.bfloat16
NT = (((1,), (1,)), ((), ()))
TN = (((0,), (0,)), ((), ()))


def call(body, out_shape, *, name, scratch=(), flops=0, moved=0):
    return pl.pallas_call(
        body,
        out_shape=out_shape,
        scratch_shapes=list(scratch),
        name=name,
        compiler_params=pltpu.CompilerParams(vmem_limit_bytes=50 * 1024 * 1024),
        cost_estimate=pl.CostEstimate(flops=flops, bytes_accessed=moved, transcendentals=0),
    )


def lane_block(shape):
    return (lax.broadcasted_iota(jnp.int32, shape, 1) // 32) % SIDE


def to_columns(rows, pick, chan):
    wide = lax.dot_general(rows, pick, TN, preferred_element_type=F32)
    block = lane_block((chan, 128))
    parts = []
    for h in range(SIDE):
        got = jnp.zeros((chan, 128), F32)
        for w in range(SIDE):
            start = (h * SIDE + w) * chan
            got = jnp.where(block == w, wide[start : start + chan, :], got)
        parts.append(got)
    return jnp.concatenate(parts, axis=1)


def to_rows(columns, pick):
    chan = columns.shape[0]
    block = lane_block((chan, 128))
    parts = []
    for h in range(SIDE):
        here = columns[:, 128 * h : 128 * h + 128]
        masked = [jnp.where(block == w, here, 0.0) for w in range(SIDE)]
        stack = jnp.concatenate(masked, axis=0).astype(BF16)
        parts.append(lax.dot_general(pick, stack, NT, preferred_element_type=F32))
    return jnp.concatenate(parts, axis=1)


def group_mean(values):
    chan, lanes = values.shape
    size = C // GROUPS
    spread = []
    for g in range(chan // size):
        total = jnp.sum(values[g * size : (g + 1) * size, :], axis=0, keepdims=True)
        folded = total[:, 0:128] + total[:, 128:256] + total[:, 256:384] + total[:, 384:512]
        folded = jnp.broadcast_to(folded, (8, 128))
        folded = folded + pltpu.roll(folded, 64, 1)
        folded = folded + pltpu.roll(folded, 32, 1)
        mean = folded[0:1, :] * (1.0 / (size * CELLS))
        wide = jnp.concatenate([mean] * SIDE, axis=1)
        spread.append(jnp.broadcast_to(wide, (size, lanes)))
    return jnp.concatenate(spread, axis=0)


def normalise(values):
    center = values - group_mean(values)
    inverse = lax.rsqrt(group_mean(center * center) + EPS)
    return center * inverse, inverse


def shift_rows(values, step):
    zero = jnp.zeros((values.shape[0], 128), values.dtype)
    if step == 0:
        return values
    if step > 0:
        return jnp.concatenate([values[:, 128:], zero], axis=1)
    return jnp.concatenate([zero, values[:, :-128]], axis=1)


def shift_columns(values, step):
    if step == 0:
        return values
    lanes = values.shape[1]
    block = lane_block(values.shape)
    moved = pltpu.roll(values, (-32 * step) % lanes, 1)
    return jnp.where((block + step >= 0) & (block + step < SIDE), moved, 0.0)


def im2col(dout, store):
    for col in range(3):
        moved = shift_columns(dout, -(col - 1)).astype(BF16)
        for row in range(3):
            store(row * 3 + col, shift_rows(moved, -(row - 1)))


def forward_kernel(rows_ref, pick_ref, gain_ref, bias_ref, maps_ref, act_ref):
    chan = act_ref.shape[0]
    maps = to_columns(rows_ref[...], pick_ref[...], chan)
    normed, _ = normalise(maps)
    shifted = normed * gain_ref[...] + bias_ref[...]
    maps_ref[...] = maps.astype(BF16)
    act_ref[...] = (shifted * jax.nn.sigmoid(shifted)).astype(BF16)


def pick_kernel(rows_ref, pick_ref, dout_ref):
    dout_ref[...] = to_columns(rows_ref[...], pick_ref[...], dout_ref.shape[0]).astype(BF16)


def back_conv_kernel(dout_ref, weight_ref, out_ref, wide_ref):
    chan = dout_ref.shape[0]

    def store(tap, rows):
        wide_ref[tap * chan : (tap + 1) * chan, :] = rows

    im2col(dout_ref[...].astype(F32), store)
    out_ref[...] = lax.dot_general(weight_ref[...], wide_ref[...], TN, preferred_element_type=F32)


def grad_weight_kernel(act_ref, dout_ref, out_ref, wide_ref):
    chan = dout_ref.shape[1]
    total = None
    for x in range(NX):

        def store(tap, rows):
            wide_ref[x, tap * chan : (tap + 1) * chan, :] = rows

        im2col(dout_ref[x].astype(F32), store)
        part = lax.dot_general(act_ref[x], wide_ref[x], NT, preferred_element_type=F32)
        total = part if total is None else total + part
    out_ref[...] = total.astype(BF16)


def conv_kernel(act_ref, weight_ref, maps_ref, table_ref, steps_ref, pick_ref, out_ref):
    chan = maps_ref.shape[0]
    conv = None
    for col in range(3):
        column = None
        for row in range(3):
            tap = row * 3 + col
            term = jnp.dot(
                weight_ref[tap * chan : (tap + 1) * chan, :], act_ref[...], preferred_element_type=F32
            )
            term = shift_rows(term, row - 1)
            column = term if column is None else column + term
        column = shift_columns(column, col - 1)
        conv = column if conv is None else conv + column
    rows = table_ref.shape[0]
    steps = steps_ref[...]
    hot = lax.broadcasted_iota(jnp.int32, (rows, 128), 0) == steps // SIDE
    wide = lax.dot_general(table_ref[...], hot.astype(BF16), TN, preferred_element_type=F32)
    embed = jnp.zeros((chan, 128), F32)
    for j in range(SIDE):
        embed = jnp.where(steps % SIDE == j, wide[j * chan : (j + 1) * chan, :], embed)
    embed = jnp.concatenate([embed] * SIDE, axis=1)
    out = maps_ref[...].astype(F32) + conv + embed
    out_ref[...] = to_rows(out, pick_ref[...]).astype(BF16)


def backward_kernel(dact_ref, maps_ref, dout_ref, gain_ref, bias_ref, pick_ref, grad_ref, sums_ref):
    gain = gain_ref[...]
    normed, inverse = normalise(maps_ref[...].astype(F32))
    shifted = normed * gain + bias_ref[...]
    gate = jax.nn.sigmoid(shifted)
    dshift = dact_ref[...] * gate * (1.0 + shifted * (1.0 - gate))
    ones = jnp.ones((8, dshift.shape[1]), F32)
    exact = lax.Precision.HIGHEST
    sums_ref[0:8, :] = lax.dot_general(ones, dshift * normed, NT, precision=exact, preferred_element_type=F32)
    sums_ref[8:16, :] = lax.dot_general(ones, dshift, NT, precision=exact, preferred_element_type=F32)
    dnormed = dshift * gain
    dmaps = inverse * (dnormed - group_mean(dnormed) - normed * group_mean(dnormed * normed))
    grad_ref[...] = to_rows(dout_ref[...].astype(F32) + dmaps, pick_ref[...]).astype(BF16)


def transpose_kernel(scale, in_ref, out_ref):
    out_ref[...] = in_ref[...].astype(F32).T * scale


def per_device(
    latents, bucket_ids, timesteps, time_table, norm_gain, norm_bias, conv_weight, cotangent
):
    dp_count = lax.axis_size("dp")
    samples, height, _, packed = latents.shape
    chan = packed // SIDE
    slots = cotangent.shape[0]
    cap = slots // dp_count
    cells = height * packed
    lanes = samples * CELLS
    along_x = [[z + NZ * x for x in range(NX)] for z in range(NZ)]
    along_z = [[z + NZ * x for z in range(NZ)] for x in range(NX)]
    scale = 1.0 / math.sqrt(samples * dp_count * CELLS)

    gain = norm_gain.reshape(chan, 1)
    bias = norm_bias.reshape(chan, 1)
    weight = conv_weight.reshape(9 * chan, C)

    same = (
        lax.broadcasted_iota(jnp.int32, (samples, 128), 0)
        == lax.broadcasted_iota(jnp.int32, (samples, 128), 1) % samples
    ).astype(BF16)
    maps, act = call(
        forward_kernel,
        (jax.ShapeDtypeStruct((chan, lanes), BF16), jax.ShapeDtypeStruct((chan, lanes), BF16)),
        name="norm_forward",
        moved=1000000,
    )(latents.reshape(samples, cells), same, gain, bias)
    act_all = lax.all_gather(act, "chan", axis=0, tiled=True)

    buckets = bucket_ids[:, 0]
    order = jnp.arange(samples, dtype=jnp.int32)
    earlier = (buckets[:, None] == buckets[None, :]) & (order[None, :] < order[:, None])
    target = buckets * cap + jnp.sum(earlier.astype(jnp.int32), axis=1)
    target = jnp.tile(target, 128 // samples)
    pick = (target[None, :] == jnp.arange(slots, dtype=jnp.int32)[:, None]).astype(BF16)

    got = lax.all_to_all(cotangent, "dp", split_axis=0, concat_axis=0, tiled=True)
    dout = call(
        pick_kernel, jax.ShapeDtypeStruct((chan, lanes), BF16), name="pick_dout", moved=1000000
    )(got.reshape(slots, cells), pick)
    dout_x = lax.all_gather(dout, "dp", axis=0, tiled=False, axis_index_groups=along_x)

    partial_dact = call(
        back_conv_kernel,
        jax.ShapeDtypeStruct((C, lanes), F32),
        name="back_conv",
        scratch=[pltpu.VMEM((9 * chan, lanes), BF16)],
        flops=2 * 9 * chan * C * lanes,
        moved=6500000,
    )(dout, weight)
    dact = lax.psum_scatter(partial_dact, "chan", scatter_dimension=0, tiled=True)

    act_x = lax.all_to_all(
        act_all, "dp", split_axis=0, concat_axis=0, tiled=True, axis_index_groups=along_x
    ).reshape(NX, C // NX, lanes)
    part = call(
        grad_weight_kernel,
        jax.ShapeDtypeStruct((C // NX, 9 * chan), BF16),
        name="grad_weight",
        scratch=[pltpu.VMEM((NX, 9 * chan, lanes), BF16)],
        flops=2 * 9 * chan * C * lanes,
        moved=4000000,
    )(act_x, dout_x)
    parts = lax.all_to_all(
        part, "dp", split_axis=0, concat_axis=0, tiled=True, axis_index_groups=along_z
    ).reshape(NZ, C // NX // NZ, 9 * chan)
    mine = jnp.sum(parts.astype(F32), axis=0).astype(BF16)
    gathered = lax.all_gather(mine, "dp", axis=0, tiled=True)

    steps = jnp.tile(timesteps, 128 // samples).reshape(1, 128)
    out_rows = call(
        conv_kernel,
        jax.ShapeDtypeStruct((slots, cells), BF16),
        name="conv",
        flops=2 * 9 * chan * C * lanes,
        moved=6500000,
    )(act_all, weight, maps, time_table.reshape(-1, packed), steps, pick)
    grad_rows, sums = call(
        backward_kernel,
        (jax.ShapeDtypeStruct((slots, cells), BF16), jax.ShapeDtypeStruct((16, chan), F32)),
        name="norm_backward",
        moved=1500000,
    )(dact, maps, dout, gain, bias, pick)

    sums = sums.reshape(2, 8, chan)[:, 0].reshape(1, 2 * chan)
    high = sums.astype(BF16)
    low = (sums - high.astype(F32)).astype(BF16)
    extra = jnp.concatenate([high, low], axis=1).reshape(1, 1, 1, packed)
    extra = jnp.broadcast_to(extra, (dp_count, 1, height, packed))
    payload = jnp.concatenate(
        [
            out_rows.reshape(dp_count, cap, height, packed),
            grad_rows.reshape(dp_count, cap, height, packed),
            extra,
        ],
        axis=1,
    )
    back = lax.all_to_all(payload, "dp", split_axis=0, concat_axis=0, tiled=True)
    out_slots = back[:, :cap].reshape(slots, height, 1, packed)
    grad_slots = back[:, cap : 2 * cap].reshape(slots, height, 1, packed)
    sent = jnp.sum(back[:, 2 * cap, 0, :].astype(F32), axis=0)
    grad_norm = (sent[: 2 * chan] + sent[2 * chan :]).reshape(2, chan) * scale

    block = 256
    grad_weight = pl.pallas_call(
        functools.partial(transpose_kernel, scale),
        grid=(C // block,),
        in_specs=[pl.BlockSpec((block, 9 * chan), lambda i: (i, 0))],
        out_specs=pl.BlockSpec((9 * chan, block), lambda i: (0, i)),
        out_shape=jax.ShapeDtypeStruct((9 * chan, C), F32),
        name="grad_weight_out",
        compiler_params=pltpu.CompilerParams(vmem_limit_bytes=40 * 1024 * 1024),
    )(gathered)
    return (out_slots, grad_slots, grad_weight.reshape(3, 3, chan, C), grad_norm)


def solution(mesh):
    in_specs = (
        P("dp", None, "chan", None),
        P("dp", None),
        P("dp"),
        P(None, "chan", None),
        P("chan"),
        P("chan"),
        P(None, None, "chan", None),
        P("dp", None, "chan", None),
    )
    out_specs = (
        P("dp", None, "chan", None),
        P("dp", None, "chan", None),
        P(None, None, "chan", None),
        P(None, "chan"),
    )
    return jax.shard_map(
        per_device, mesh=mesh, in_specs=in_specs, out_specs=out_specs, check_vma=False
    )
```

```python
import functools
import math

import jax
import jax.numpy as jnp
from jax import lax
from jax.experimental import pallas as pl
from jax.experimental.pallas import tpu as pltpu
from jax.sharding import PartitionSpec as P

C = 1280
GROUPS = 32
SIDE = 4
CELLS = 16
EPS = 1e-05
NX = 4
NZ = 8
F32 = jnp.float32
BF16 = jnp.bfloat16
NT = (((1,), (1,)), ((), ()))
TN = (((0,), (0,)), ((), ()))


def lane_block(shape):
    return (lax.broadcasted_iota(jnp.int32, shape, 1) // 32) % SIDE


def to_columns(rows, pick, chan):
    wide = lax.dot_general(rows, pick, TN, preferred_element_type=F32)
    block = lane_block((chan, 128))
    parts = []
    for h in range(SIDE):
        got = jnp.zeros((chan, 128), F32)
        for w in range(SIDE):
            start = (h * SIDE + w) * chan
            got = jnp.where(block == w, wide[start : start + chan, :], got)
        parts.append(got)
    return jnp.concatenate(parts, axis=1)


def to_rows(columns, pick):
    chan = columns.shape[0]
    block = lane_block((chan, 128))
    parts = []
    for h in range(SIDE):
        here = columns[:, 128 * h : 128 * h + 128]
        masked = [jnp.where(block == w, here, 0.0) for w in range(SIDE)]
        stack = jnp.concatenate(masked, axis=0).astype(BF16)
        parts.append(lax.dot_general(pick, stack, NT, preferred_element_type=F32))
    return jnp.concatenate(parts, axis=1)


def group_mean(values):
    chan, lanes = values.shape
    size = C // GROUPS
    spread = []
    for g in range(chan // size):
        total = jnp.sum(values[g * size : (g + 1) * size, :], axis=0, keepdims=True)
        folded = total[:, 0:128] + total[:, 128:256] + total[:, 256:384] + total[:, 384:512]
        folded = jnp.broadcast_to(folded, (8, 128))
        folded = folded + pltpu.roll(folded, 64, 1)
        folded = folded + pltpu.roll(folded, 32, 1)
        mean = folded[0:1, :] * (1.0 / (size * CELLS))
        wide = jnp.concatenate([mean] * SIDE, axis=1)
        spread.append(jnp.broadcast_to(wide, (size, lanes)))
    return jnp.concatenate(spread, axis=0)


def normalise(values):
    center = values - group_mean(values)
    inverse = lax.rsqrt(group_mean(center * center) + EPS)
    return center * inverse, inverse


def shift_rows(values, step):
    zero = jnp.zeros((values.shape[0], 128), values.dtype)
    if step == 0:
        return values
    if step > 0:
        return jnp.concatenate([values[:, 128:], zero], axis=1)
    return jnp.concatenate([zero, values[:, :-128]], axis=1)


def shift_columns(values, step):
    if step == 0:
        return values
    lanes = values.shape[1]
    block = lane_block(values.shape)
    moved = pltpu.roll(values, (-32 * step) % lanes, 1)
    return jnp.where((block + step >= 0) & (block + step < SIDE), moved, 0.0)


def im2col(dout, store):
    for col in range(3):
        moved = shift_columns(dout, -(col - 1)).astype(BF16)
        for row in range(3):
            store(row * 3 + col, shift_rows(moved, -(row - 1)))


def column(row):
    n = row.shape[1]
    eye = lax.broadcasted_iota(jnp.int32, (n, n), 0) == lax.broadcasted_iota(jnp.int32, (n, n), 1)
    return jnp.sum(jnp.where(eye, jnp.broadcast_to(row, (n, n)), 0.0), axis=1, keepdims=True)


def forward_kernel(rows_ref, pick_ref, gain_ref, bias_ref, maps_ref, act_ref):
    chan = act_ref.shape[0]
    maps = to_columns(rows_ref[...], pick_ref[...], chan)
    normed, _ = normalise(maps)
    shifted = normed * column(gain_ref[...]) + column(bias_ref[...])
    maps_ref[...] = maps.astype(BF16)
    act_ref[...] = (shifted * jax.nn.sigmoid(shifted)).astype(BF16)


def place_act_kernel(where_ref, own_ref, a_ref, b_ref, c_ref, other_ref, all_ref, slices_ref):
    chan = own_ref.shape[0]

    def put(block, value):
        all_ref[pl.ds(pl.multiple_of(block * chan, 32), chan), :] = value

    for j, ref in enumerate((own_ref, a_ref, b_ref, c_ref)):
        put(where_ref[j], ref[...])
        put(where_ref[4 + j], other_ref[j])
    for x in range(NX):
        slices_ref[x, 0:256, :] = all_ref[256 * x : 256 * x + 256, :]
        slices_ref[x, 256:320, :] = all_ref[1024 + 64 * x : 1088 + 64 * x, :]


def pick_kernel(rows_ref, pick_ref, dout_ref):
    dout_ref[...] = to_columns(rows_ref[...], pick_ref[...], dout_ref.shape[0]).astype(BF16)


def back_conv_kernel(where_ref, dout_ref, weight_ref, keep_ref, give_ref, wide_ref, full_ref):
    chan = dout_ref.shape[0]

    def store(tap, rows):
        wide_ref[tap * chan : (tap + 1) * chan, :] = rows

    im2col(dout_ref[...].astype(F32), store)
    full_ref[...] = lax.dot_general(weight_ref[...], wide_ref[...], TN, preferred_element_type=F32)
    for j in range(4):
        keep_ref[j] = full_ref[pl.ds(pl.multiple_of(where_ref[j] * chan, 32), chan), :]
        give_ref[j] = full_ref[pl.ds(pl.multiple_of(where_ref[4 + j] * chan, 32), chan), :]


def add_kernel(keep_ref, got_ref, *out_refs):
    for j, ref in enumerate(out_refs):
        ref[...] = keep_ref[j] + got_ref[j]


def grad_weight_kernel(x_ref, z_ref, act_ref, *refs):
    douts, outs, (wide_ref, total_ref) = refs[:NX], refs[NX : NX + NZ], refs[NX + NZ :]
    chan = douts[0].shape[0]
    total = None
    for k in range(NX):

        def store(tap, rows):
            wide_ref[k, tap * chan : (tap + 1) * chan, :] = rows

        im2col(douts[k][...].astype(F32), store)
        part = lax.dot_general(act_ref[x_ref[k]], wide_ref[k], NT, preferred_element_type=F32)
        total = part if total is None else total + part
    total_ref[...] = total
    size = outs[0].shape[0]
    for k in range(NZ):
        start = pl.multiple_of(z_ref[k] * size, 8)
        outs[k][...] = total_ref[pl.ds(start, size), :].astype(outs[k].dtype)


def place_z_kernel(z_ref, *refs):
    out_ref = refs[-1]
    for k in range(7):
        out_ref[z_ref[k]] = refs[k][...]
    out_ref[z_ref[7]] = jnp.concatenate([refs[7][...], refs[8][...]], axis=0)


def conv_kernel(act_ref, weight_ref, maps_ref, table_ref, steps_ref, pick_ref, out_ref):
    chan = maps_ref.shape[0]
    conv = None
    for col in range(3):
        column_sum = None
        for row in range(3):
            tap = row * 3 + col
            term = jnp.dot(
                weight_ref[tap * chan : (tap + 1) * chan, :], act_ref[...], preferred_element_type=F32
            )
            term = shift_rows(term, row - 1)
            column_sum = term if column_sum is None else column_sum + term
        column_sum = shift_columns(column_sum, col - 1)
        conv = column_sum if conv is None else conv + column_sum
    rows = table_ref.shape[0]
    steps = steps_ref[...]
    hot = lax.broadcasted_iota(jnp.int32, (rows, 128), 0) == steps // SIDE
    wide = lax.dot_general(table_ref[...], hot.astype(BF16), TN, preferred_element_type=F32)
    embed = jnp.zeros((chan, 128), F32)
    for j in range(SIDE):
        embed = jnp.where(steps % SIDE == j, wide[j * chan : (j + 1) * chan, :], embed)
    embed = jnp.concatenate([embed] * SIDE, axis=1)
    out = maps_ref[...].astype(F32) + conv + embed
    out_ref[...] = to_rows(out, pick_ref[...]).astype(BF16)


def backward_kernel(
    own_ref, a_ref, b_ref, c_ref, maps_ref, dout_ref, gain_ref, bias_ref, pick_ref, grad_ref, sums_ref
):
    gain = column(gain_ref[...])
    dact = own_ref[...] + a_ref[...] + b_ref[...] + c_ref[...]
    normed, inverse = normalise(maps_ref[...].astype(F32))
    shifted = normed * gain + column(bias_ref[...])
    gate = jax.nn.sigmoid(shifted)
    dshift = dact * gate * (1.0 + shifted * (1.0 - gate))
    ones = jnp.ones((8, dshift.shape[1]), F32)
    exact = lax.Precision.HIGHEST
    sums_ref[0:8, :] = lax.dot_general(ones, dshift * normed, NT, precision=exact, preferred_element_type=F32)
    sums_ref[8:16, :] = lax.dot_general(ones, dshift, NT, precision=exact, preferred_element_type=F32)
    dnormed = dshift * gain
    dmaps = inverse * (dnormed - group_mean(dnormed) - normed * group_mean(dnormed * normed))
    grad_ref[...] = to_rows(dout_ref[...].astype(F32) + dmaps, pick_ref[...]).astype(BF16)


def finish_kernel(scale, x_ref, own_ref, left_ref, right_ref, low_ref, high_ref, out_ref, tail_ref):
    def flat(ref):
        value = ref[...].astype(F32)
        return value.reshape(value.shape[0] * value.shape[1], value.shape[2])

    pieces = [flat(own_ref), flat(left_ref), flat(right_ref), jnp.concatenate([flat(low_ref), flat(high_ref)], axis=0)]
    for k, piece in enumerate(pieces):
        out_ref[:, pl.ds(pl.multiple_of(x_ref[k] * 256, 256), 256)] = piece[0:256].T * scale
        tail_ref[pl.ds(pl.multiple_of(x_ref[k] * 64, 64), 64), :] = piece[256:320]
    out_ref[:, 1024:1280] = tail_ref[...].T * scale


def per_device(
    latents, bucket_ids, timesteps, time_table, norm_gain, norm_bias, conv_weight, cotangent
):
    dp_count = lax.axis_size("dp")
    samples, height, _, packed = latents.shape
    chan = packed // SIDE
    slots = cotangent.shape[0]
    cap = slots // dp_count
    cells = height * packed
    lanes = samples * CELLS
    wide = 9 * chan
    piece = C // NX // NZ
    along_x = [[z + NZ * x for x in range(NX)] for z in range(NZ)]
    scale = 1.0 / math.sqrt(samples * dp_count * CELLS)
    place = lax.axis_index("dp")
    x, z = place // NZ, place % NZ
    mine_chan = lax.axis_index("chan")
    y, core = mine_chan // 2, mine_chan % 2
    vmem = pl.BlockSpec(memory_space=pltpu.VMEM)
    smem = pl.BlockSpec(memory_space=pltpu.SMEM)

    def move(value, dx, dz):
        pairs = [
            (i * NZ + j, (i + dx) % NX * NZ + (j + dz) % NZ) for i in range(NX) for j in range(NZ)
        ]
        return lax.ppermute(value, "dp", pairs)

    def move_chan(value, dy, flip):
        pairs = [(i * 2 + j, (i + dy) % 4 * 2 + (j ^ flip)) for i in range(4) for j in range(2)]
        return lax.ppermute(value, "chan", pairs)

    def kernel(body, out_shape, scalars, operands, name, scratch=(), flops=0, moved=1000000):
        return pl.pallas_call(
            body,
            in_specs=[smem] * len(scalars) + [vmem] * len(operands),
            out_shape=out_shape,
            scratch_shapes=list(scratch),
            name=name,
            compiler_params=pltpu.CompilerParams(vmem_limit_bytes=50 * 1024 * 1024),
            cost_estimate=pl.CostEstimate(flops=flops, bytes_accessed=moved, transcendentals=0),
        )(*scalars, *operands)

    def shape(*dims, dtype=BF16):
        return jax.ShapeDtypeStruct(dims, dtype)

    steps_y = jnp.array([0, 1, 3, 2], jnp.int32)
    to_y = (y + steps_y) % 4 * 2
    from_y = (y - steps_y) % 4 * 2
    give_where = jnp.concatenate([to_y + core, to_y + 1 - core])
    act_where = jnp.concatenate([from_y + core, from_y + 1 - core])
    x_from = (x - jnp.arange(NX, dtype=jnp.int32)) % NX
    z_to = (z + jnp.arange(NZ, dtype=jnp.int32)) % NZ
    z_ring = (z + jnp.array([0, -1, 1, -2, 2, -3, 3, 4], jnp.int32)) % NZ
    x_ring = (x + jnp.array([0, -1, 1, 2], jnp.int32)) % NX

    gain = norm_gain.reshape(1, chan)
    bias = norm_bias.reshape(1, chan)
    weight = conv_weight.reshape(wide, C)

    same = (
        lax.broadcasted_iota(jnp.int32, (samples, 128), 0)
        == lax.broadcasted_iota(jnp.int32, (samples, 128), 1) % samples
    ).astype(BF16)
    maps, act = kernel(
        forward_kernel,
        (shape(chan, lanes), shape(chan, lanes)),
        (),
        (latents.reshape(samples, cells), same, gain, bias),
        "norm_forward",
    )
    near = [move_chan(act, 1, 0), move_chan(act, -1, 0), move_chan(act, 2, 0)]
    other = move_chan(jnp.stack([act] + near), 0, 1)
    act_all, act_slices = kernel(
        place_act_kernel,
        (shape(C, lanes), shape(NX, C // NX, lanes)),
        (act_where,),
        (act, *near, other),
        "place_act",
    )
    act_x = lax.all_to_all(
        act_slices, "dp", split_axis=0, concat_axis=0, tiled=True, axis_index_groups=along_x
    )

    buckets = bucket_ids[:, 0]
    order = jnp.arange(samples, dtype=jnp.int32)
    earlier = (buckets[:, None] == buckets[None, :]) & (order[None, :] < order[:, None])
    target = buckets * cap + jnp.sum(earlier.astype(jnp.int32), axis=1)
    target = jnp.tile(target, 128 // samples)
    pick = (target[None, :] == jnp.arange(slots, dtype=jnp.int32)[:, None]).astype(BF16)

    got = lax.all_to_all(cotangent, "dp", split_axis=0, concat_axis=0, tiled=True)
    dout = kernel(pick_kernel, shape(chan, lanes), (), (got.reshape(slots, cells), pick), "pick_dout")
    douts = [dout] + [move(dout, k, 0) for k in range(1, NX)]

    keep, give = kernel(
        back_conv_kernel,
        (shape(4, chan, lanes, dtype=F32), shape(4, chan, lanes, dtype=F32)),
        (give_where,),
        (dout, weight),
        "back_conv",
        scratch=[pltpu.VMEM((wide, lanes), BF16), pltpu.VMEM((C, lanes), F32)],
        flops=2 * wide * C * lanes,
        moved=6500000,
    )
    sums = kernel(
        add_kernel, tuple(shape(chan, lanes, dtype=F32) for _ in range(4)), (), (keep, move_chan(give, 0, 1)), "add_cores"
    )
    dacts = [sums[0], move_chan(sums[1], 1, 0), move_chan(sums[2], -1, 0), move_chan(sums[3], 2, 0)]

    chunks = kernel(
        grad_weight_kernel,
        (shape(piece, wide, dtype=F32),) + tuple(shape(piece, wide) for _ in range(NZ - 1)),
        (x_from, z_to),
        (act_x, *douts),
        "grad_weight",
        scratch=[pltpu.VMEM((NX, wide, lanes), BF16), pltpu.VMEM((C // NX, wide), F32)],
        flops=2 * wide * C * lanes,
        moved=4000000,
    )
    total = chunks[0]
    for k in range(1, NZ):
        total = total + move(chunks[k], 0, k).astype(F32)
    mine = total.astype(BF16)
    up = down = mine
    ring = [mine]
    for _ in range(3):
        up, down = move(up, 0, 1), move(down, 0, -1)
        ring += [up, down]
    ring += [move(up[:16], 0, 1), move(down[16:], 0, -1)]
    block = kernel(place_z_kernel, shape(NZ, piece, wide), (z_ring,), tuple(ring), "place_z")
    left, right = move(block, 1, 0), move(block, -1, 0)
    half = NZ // 2
    low, high = move(left[:half], 1, 0), move(right[half:], -1, 0)

    steps = jnp.tile(timesteps, 128 // samples).reshape(1, 128)
    out_rows = kernel(
        conv_kernel,
        shape(slots, cells),
        (),
        (act_all, weight, maps, time_table.reshape(-1, packed), steps, pick),
        "conv",
        flops=2 * wide * C * lanes,
        moved=6500000,
    )
    grad_rows, stats = kernel(
        backward_kernel,
        (shape(slots, cells), shape(16, chan, dtype=F32)),
        (),
        (*dacts, maps, dout, gain, bias, pick),
        "norm_backward",
    )

    stats = stats.reshape(2, 8, chan)[:, 0].reshape(1, 2 * chan)
    upper = stats.astype(BF16)
    lower = (stats - upper.astype(F32)).astype(BF16)
    extra = jnp.concatenate([upper, lower], axis=1).reshape(1, 1, 1, packed)
    extra = jnp.broadcast_to(extra, (dp_count, 1, height, packed))
    payload = jnp.concatenate(
        [
            out_rows.reshape(dp_count, cap, height, packed),
            grad_rows.reshape(dp_count, cap, height, packed),
            extra,
        ],
        axis=1,
    )
    back = lax.all_to_all(payload, "dp", split_axis=0, concat_axis=0, tiled=True)
    out_slots = back[:, :cap].reshape(slots, height, 1, packed)
    grad_slots = back[:, cap : 2 * cap].reshape(slots, height, 1, packed)
    sent = jnp.sum(back[:, 2 * cap, 0, :].astype(F32), axis=0)
    grad_norm = (sent[: 2 * chan] + sent[2 * chan :]).reshape(2, chan) * scale

    width = 256
    full = pl.BlockSpec((NZ, piece, width), lambda i: (0, 0, i))
    part = pl.BlockSpec((half, piece, width), lambda i: (0, 0, i))
    grad_weight = pl.pallas_call(
        functools.partial(finish_kernel, scale),
        grid=(pl.cdiv(wide, width),),
        in_specs=[smem, full, full, full, part, part],
        out_specs=pl.BlockSpec((width, C), lambda i: (i, 0)),
        out_shape=jax.ShapeDtypeStruct((wide, C), F32),
        scratch_shapes=[pltpu.VMEM((256, width), F32)],
        name="grad_weight_out",
        compiler_params=pltpu.CompilerParams(vmem_limit_bytes=40 * 1024 * 1024),
    )(x_ring, block, left, right, low, high)
    return (out_slots, grad_slots, grad_weight.reshape(3, 3, chan, C), grad_norm)


def solution(mesh):
    in_specs = (
        P("dp", None, "chan", None),
        P("dp", None),
        P("dp"),
        P(None, "chan", None),
        P("chan"),
        P("chan"),
        P(None, None, "chan", None),
        P("dp", None, "chan", None),
    )
    out_specs = (
        P("dp", None, "chan", None),
        P("dp", None, "chan", None),
        P(None, None, "chan", None),
        P(None, "chan"),
    )
    return jax.shard_map(
        per_device, mesh=mesh, in_specs=in_specs, out_specs=out_specs, check_vma=False
    )
```

```python
import functools
import math

import jax
import jax.numpy as jnp
from jax import lax
from jax.experimental import pallas as pl
from jax.experimental.pallas import tpu as pltpu
from jax.sharding import PartitionSpec as P

C = 1280
GROUPS = 32
SIDE = 4
CELLS = 16
EPS = 1e-05
NX = 4
NZ = 8
F32 = jnp.float32
BF16 = jnp.bfloat16
NT = (((1,), (1,)), ((), ()))
TN = (((0,), (0,)), ((), ()))


def lane_block(shape):
    return (lax.broadcasted_iota(jnp.int32, shape, 1) // 32) % SIDE


def to_columns(rows, pick, chan):
    wide = lax.dot_general(rows, pick, TN, preferred_element_type=F32)
    block = lane_block((chan, 128))
    parts = []
    for h in range(SIDE):
        got = jnp.zeros((chan, 128), F32)
        for w in range(SIDE):
            start = (h * SIDE + w) * chan
            got = jnp.where(block == w, wide[start : start + chan, :], got)
        parts.append(got)
    return jnp.concatenate(parts, axis=1)


def to_rows(columns, pick):
    chan = columns.shape[0]
    block = lane_block((chan, 128))
    parts = []
    for h in range(SIDE):
        here = columns[:, 128 * h : 128 * h + 128]
        masked = [jnp.where(block == w, here, 0.0) for w in range(SIDE)]
        stack = jnp.concatenate(masked, axis=0).astype(BF16)
        parts.append(lax.dot_general(pick, stack, NT, preferred_element_type=F32))
    return jnp.concatenate(parts, axis=1)


def group_mean(values):
    chan, lanes = values.shape
    size = C // GROUPS
    spread = []
    for g in range(chan // size):
        total = jnp.sum(values[g * size : (g + 1) * size, :], axis=0, keepdims=True)
        folded = total[:, 0:128] + total[:, 128:256] + total[:, 256:384] + total[:, 384:512]
        folded = jnp.broadcast_to(folded, (8, 128))
        folded = folded + pltpu.roll(folded, 64, 1)
        folded = folded + pltpu.roll(folded, 32, 1)
        mean = folded[0:1, :] * (1.0 / (size * CELLS))
        wide = jnp.concatenate([mean] * SIDE, axis=1)
        spread.append(jnp.broadcast_to(wide, (size, lanes)))
    return jnp.concatenate(spread, axis=0)


def normalise(values):
    center = values - group_mean(values)
    inverse = lax.rsqrt(group_mean(center * center) + EPS)
    return center * inverse, inverse


def shift_rows(values, step):
    zero = jnp.zeros((values.shape[0], 128), values.dtype)
    if step == 0:
        return values
    if step > 0:
        return jnp.concatenate([values[:, 128:], zero], axis=1)
    return jnp.concatenate([zero, values[:, :-128]], axis=1)


def shift_columns(values, step):
    if step == 0:
        return values
    lanes = values.shape[1]
    block = lane_block(values.shape)
    moved = pltpu.roll(values, (-32 * step) % lanes, 1)
    return jnp.where((block + step >= 0) & (block + step < SIDE), moved, 0.0)


def im2col(dout, store):
    for col in range(3):
        moved = shift_columns(dout, -(col - 1)).astype(BF16)
        for row in range(3):
            store(row * 3 + col, shift_rows(moved, -(row - 1)))


def column(row):
    n = row.shape[1]
    eye = lax.broadcasted_iota(jnp.int32, (n, n), 0) == lax.broadcasted_iota(jnp.int32, (n, n), 1)
    return jnp.sum(jnp.where(eye, jnp.broadcast_to(row, (n, n)), 0.0), axis=1, keepdims=True)


def forward_kernel(rows_ref, pick_ref, gain_ref, bias_ref, maps_ref, act_ref):
    chan = act_ref.shape[0]
    maps = to_columns(rows_ref[...], pick_ref[...], chan)
    normed, _ = normalise(maps)
    shifted = normed * column(gain_ref[...]) + column(bias_ref[...])
    maps_ref[...] = maps.astype(BF16)
    act_ref[...] = (shifted * jax.nn.sigmoid(shifted)).astype(BF16)


def place_act_kernel(where_ref, x_ref, core_ref, own_ref, a_ref, b_ref, c_ref, other_ref, all_ref, home_ref, *halves):
    chan = own_ref.shape[0]

    def put(block, value):
        all_ref[pl.ds(pl.multiple_of(block * chan, 32), chan), :] = value

    for j, ref in enumerate((own_ref, a_ref, b_ref, c_ref)):
        put(where_ref[j], ref[...])
        put(where_ref[4 + j], other_ref[j])

    def rows(start, size):
        return all_ref[pl.ds(pl.multiple_of(start, 32), size), :]

    home_ref[0:256, :] = rows(256 * x_ref[0], 256)
    home_ref[256:320, :] = rows(1024 + 64 * x_ref[0], 64)
    for core in range(2):

        @pl.when(core_ref[0] == core)
        def _():
            for k, ref in enumerate(halves):
                x = x_ref[k + 1]
                if core == 0:
                    ref[...] = rows(256 * x, 160)
                else:
                    ref[0:96, :] = rows(256 * x + 160, 96)
                    ref[96:160, :] = rows(1024 + 64 * x, 64)


def pick_kernel(rows_ref, pick_ref, _, dout_ref):
    dout_ref[...] = to_columns(rows_ref[...], pick_ref[...], dout_ref.shape[0]).astype(BF16)


def back_conv_kernel(where_ref, dout_ref, weight_ref, _, keep_ref, give_ref, wide_ref, full_ref):
    chan = dout_ref.shape[0]

    def store(tap, rows):
        wide_ref[tap * chan : (tap + 1) * chan, :] = rows

    im2col(dout_ref[...].astype(F32), store)
    full_ref[...] = lax.dot_general(weight_ref[...], wide_ref[...], TN, preferred_element_type=F32)
    for j in range(4):
        keep_ref[j] = full_ref[pl.ds(pl.multiple_of(where_ref[j] * chan, 32), chan), :]
        give_ref[j] = full_ref[pl.ds(pl.multiple_of(where_ref[4 + j] * chan, 32), chan), :]


def add_kernel(keep_ref, got_ref, *out_refs):
    for j, ref in enumerate(out_refs):
        ref[...] = keep_ref[j] + got_ref[j]


def grad_weight_kernel(core_ref, z_ref, home_ref, other_ref, *refs):
    near, (dout_ref, left_ref, low_ref, high_ref, right_ref) = refs[: NX - 1], refs[NX - 1 : NX + 4]
    outs, (act_ref, wide_ref, total_ref) = refs[NX + 4 : -3], refs[-3:]
    chan = dout_ref.shape[0]
    across = jnp.concatenate([low_ref[...].astype(F32), high_ref[...].astype(F32)], axis=0)
    douts = [dout_ref[...].astype(F32), left_ref[...].astype(F32), across, right_ref[...].astype(F32)]
    half = near[0].shape[0]
    mine = pl.multiple_of(core_ref[0] * half, 32)
    rest = pl.multiple_of((1 - core_ref[0]) * half, 32)
    total = None
    for k in range(NX):

        def store(tap, rows):
            wide_ref[k, tap * chan : (tap + 1) * chan, :] = rows

        im2col(douts[k], store)
        if k:
            act_ref[k - 1, pl.ds(mine, half), :] = near[k - 1][...]
            act_ref[k - 1, pl.ds(rest, half), :] = other_ref[k - 1]
        act = act_ref[k - 1] if k else home_ref[...]
        part = lax.dot_general(act, wide_ref[k], NT, preferred_element_type=F32)
        total = part if total is None else total + part
    total_ref[...] = total
    size = outs[0].shape[0]
    for k in range(NZ):
        start = pl.multiple_of(z_ref[k] * size, 8)
        outs[k][...] = total_ref[pl.ds(start, size), :].astype(outs[k].dtype)


def sum_kernel(_, own_ref, *refs):
    total = own_ref[...]
    for ref in refs[:-1]:
        total = total + ref[...].astype(F32)
    refs[-1][...] = total.astype(BF16)


def conv_kernel(act_ref, weight_ref, maps_ref, table_ref, steps_ref, pick_ref, _, out_ref):
    chan = maps_ref.shape[0]
    conv = None
    for col in range(3):
        column_sum = None
        for row in range(3):
            tap = row * 3 + col
            term = jnp.dot(
                weight_ref[tap * chan : (tap + 1) * chan, :], act_ref[...], preferred_element_type=F32
            )
            term = shift_rows(term, row - 1)
            column_sum = term if column_sum is None else column_sum + term
        column_sum = shift_columns(column_sum, col - 1)
        conv = column_sum if conv is None else conv + column_sum
    rows = table_ref.shape[0]
    steps = steps_ref[...]
    hot = lax.broadcasted_iota(jnp.int32, (rows, 128), 0) == steps // SIDE
    wide = lax.dot_general(table_ref[...], hot.astype(BF16), TN, preferred_element_type=F32)
    embed = jnp.zeros((chan, 128), F32)
    for j in range(SIDE):
        embed = jnp.where(steps % SIDE == j, wide[j * chan : (j + 1) * chan, :], embed)
    embed = jnp.concatenate([embed] * SIDE, axis=1)
    out = maps_ref[...].astype(F32) + conv + embed
    out_ref[...] = to_rows(out, pick_ref[...]).astype(BF16)


def backward_kernel(
    own_ref, a_ref, b_ref, c_ref, maps_ref, dout_ref, gain_ref, bias_ref, pick_ref, grad_ref, sums_ref
):
    gain = column(gain_ref[...])
    dact = own_ref[...] + a_ref[...] + b_ref[...] + c_ref[...]
    normed, inverse = normalise(maps_ref[...].astype(F32))
    shifted = normed * gain + column(bias_ref[...])
    gate = jax.nn.sigmoid(shifted)
    dshift = dact * gate * (1.0 + shifted * (1.0 - gate))
    ones = jnp.ones((8, dshift.shape[1]), F32)
    exact = lax.Precision.HIGHEST
    sums_ref[0:8, :] = lax.dot_general(ones, dshift * normed, NT, precision=exact, preferred_element_type=F32)
    sums_ref[8:16, :] = lax.dot_general(ones, dshift, NT, precision=exact, preferred_element_type=F32)
    dnormed = dshift * gain
    dmaps = inverse * (dnormed - group_mean(dnormed) - normed * group_mean(dnormed * normed))
    grad_ref[...] = to_rows(dout_ref[...].astype(F32) + dmaps, pick_ref[...]).astype(BF16)


def finish_kernel(scale, x_ref, z_ref, *refs):
    sources, (out_ref, slice_ref, tail_ref) = refs[:-3], refs[-3:]
    size = sources[0].shape[1]
    pieces = [[(ref, j) for ref in group for j in range(ref.shape[0])] for group in (sources[0:2], sources[2:4], sources[4:6], sources[6:10])]
    for k, blocks in enumerate(pieces):
        for j, (ref, at) in enumerate(blocks):
            slice_ref[pl.ds(pl.multiple_of(z_ref[j] * size, 8), size), :] = ref[at].astype(F32)
        out_ref[:, pl.ds(pl.multiple_of(x_ref[k] * 256, 256), 256)] = slice_ref[0:256, :].T * scale
        tail_ref[pl.ds(pl.multiple_of(x_ref[k] * 64, 64), 64), :] = slice_ref[256:320, :]
    out_ref[:, 1024:1280] = tail_ref[...].T * scale


def per_device(
    latents, bucket_ids, timesteps, time_table, norm_gain, norm_bias, conv_weight, cotangent
):
    dp_count = lax.axis_size("dp")
    samples, height, _, packed = latents.shape
    chan = packed // SIDE
    slots = cotangent.shape[0]
    cap = slots // dp_count
    cells = height * packed
    lanes = samples * CELLS
    wide = 9 * chan
    piece = C // NX // NZ
    scale = 1.0 / math.sqrt(samples * dp_count * CELLS)
    place = lax.axis_index("dp")
    x, z = place // NZ, place % NZ
    mine_chan = lax.axis_index("chan")
    y, core = mine_chan // 2, mine_chan % 2
    vmem = pl.BlockSpec(memory_space=pltpu.VMEM)
    smem = pl.BlockSpec(memory_space=pltpu.SMEM)
    anywhere = pl.BlockSpec(memory_space=pl.ANY)

    def move(value, dx, dz):
        pairs = [
            (i * NZ + j, (i + dx) % NX * NZ + (j + dz) % NZ) for i in range(NX) for j in range(NZ)
        ]
        return lax.ppermute(value, "dp", pairs)

    def move_chan(value, dy, flip):
        pairs = [(i * 2 + j, (i + dy) % 4 * 2 + (j ^ flip)) for i in range(4) for j in range(2)]
        return lax.ppermute(value, "chan", pairs)

    def kernel(body, out_shape, scalars, operands, name, scratch=(), vmem_mib=12, after=None):
        specs = [smem] * len(scalars) + [vmem] * len(operands)
        operands = list(operands)
        if after is not None:
            specs.insert(len(scalars) + after[0], anywhere)
            operands.insert(after[0], after[1])
        return pl.pallas_call(
            body,
            in_specs=specs,
            out_shape=out_shape,
            scratch_shapes=list(scratch),
            name=name,
            compiler_params=pltpu.CompilerParams(vmem_limit_bytes=vmem_mib * 1024 * 1024),
            cost_estimate=pl.CostEstimate(flops=1000, bytes_accessed=1000, transcendentals=0),
        )(*scalars, *operands)

    def shape(*dims, dtype=BF16):
        return jax.ShapeDtypeStruct(dims, dtype)

    steps_y = jnp.array([0, 1, 3, 2], jnp.int32)
    to_y = (y + steps_y) % 4 * 2
    from_y = (y - steps_y) % 4 * 2
    give_where = jnp.concatenate([to_y + core, to_y + 1 - core])
    act_where = jnp.concatenate([from_y + core, from_y + 1 - core])
    x_to = (x + jnp.arange(NX, dtype=jnp.int32)) % NX
    core_at = core.reshape(1)
    z_to = (z + jnp.arange(NZ, dtype=jnp.int32)) % NZ
    z_ring = (z + jnp.array([0, -1, 1, -2, 2, -3, 3, 4], jnp.int32)) % NZ
    x_ring = (x + jnp.array([0, -1, 1, 2], jnp.int32)) % NX

    gain = norm_gain.reshape(1, chan)
    bias = norm_bias.reshape(1, chan)
    weight = conv_weight.reshape(wide, C)

    same = (
        lax.broadcasted_iota(jnp.int32, (samples, 128), 0)
        == lax.broadcasted_iota(jnp.int32, (samples, 128), 1) % samples
    ).astype(BF16)
    maps, act = kernel(
        forward_kernel,
        (shape(chan, lanes), shape(chan, lanes)),
        (),
        (latents.reshape(samples, cells), same, gain, bias),
        "norm_forward",
    )
    near = [move_chan(act, 1, 0), move_chan(act, -1, 0), move_chan(act, 2, 0)]
    other = move_chan(jnp.stack([act] + near), 0, 1)
    act_all, act_home, *act_halves = kernel(
        place_act_kernel,
        (shape(C, lanes), shape(C // NX, lanes)) + (shape(C // NX // 2, lanes),) * (NX - 1),
        (act_where, x_to, core_at),
        (act, *near, other),
        "place_act",
    )
    act_near = [move(act_halves[k - 1], k, 0) for k in range(1, NX)]

    buckets = bucket_ids[:, 0]
    order = jnp.arange(samples, dtype=jnp.int32)
    earlier = (buckets[:, None] == buckets[None, :]) & (order[None, :] < order[:, None])
    target = buckets * cap + jnp.sum(earlier.astype(jnp.int32), axis=1)
    target = jnp.tile(target, 128 // samples)
    pick = (target[None, :] == jnp.arange(slots, dtype=jnp.int32)[:, None]).astype(BF16)

    got = lax.all_to_all(cotangent, "dp", split_axis=0, concat_axis=0, tiled=True)
    dout = kernel(pick_kernel, shape(chan, lanes), (), (got.reshape(slots, cells), pick), "pick_dout", after=(2, act_near[2]))
    dout_left, dout_right = move(dout, 1, 0), move(dout, -1, 0)
    *act_near, dout_left = lax.optimization_barrier((*act_near, dout_left))
    act_other = move_chan(jnp.stack(act_near), 0, 1)
    half_chan = chan // 2
    dout_low, dout_high = move(dout_left[:half_chan], 1, 0), move(dout_right[half_chan:], -1, 0)

    chunks = kernel(
        grad_weight_kernel,
        (shape(piece, wide, dtype=F32),) + tuple(shape(piece, wide) for _ in range(NZ - 1)),
        (core_at, z_to),
        (act_home, act_other, *act_near, dout, dout_left, dout_low, dout_high, dout_right),
        "grad_weight",
        scratch=[
            pltpu.VMEM((NX - 1, C // NX, lanes), BF16),
            pltpu.VMEM((NX, wide, lanes), BF16),
            pltpu.VMEM((C // NX, wide), F32),
        ],
        vmem_mib=28,
    )
    came = [move(chunks[k], 0, k) for k in range(1, NZ)]
    keep, give = kernel(
        back_conv_kernel,
        (shape(4, chan, lanes, dtype=F32), shape(4, chan, lanes, dtype=F32)),
        (give_where,),
        (dout, weight),
        "back_conv",
        scratch=[pltpu.VMEM((wide, lanes), BF16), pltpu.VMEM((C, lanes), F32)],
        vmem_mib=24,
        after=(2, came[0]),
    )
    sums = kernel(
        add_kernel, tuple(shape(chan, lanes, dtype=F32) for _ in range(4)), (), (keep, move_chan(give, 0, 1)), "add_cores"
    )
    dacts = [sums[0], move_chan(sums[1], 1, 0), move_chan(sums[2], -1, 0), move_chan(sums[3], 2, 0)]

    mine = kernel(
        sum_kernel, shape(piece, wide), (), (chunks[0], *came), "sum_z", after=(0, sums[0])
    )
    up, down = move(mine, 0, 1), move(mine, 0, -1)
    first = jnp.stack([mine, up, down])
    first_left, first_right = move(first, 1, 0), move(first, -1, 0)
    first_low, first_high = move(first_left[:2], 1, 0), move(first_right[2:], -1, 0)
    up, down = move(up, 0, 1), move(down, 0, -1)
    ring = [up, down]
    up, down, first_left, first_right, *dacts = lax.optimization_barrier(
        (up, down, first_left, first_right, *dacts)
    )
    up, down = move(up, 0, 1), move(down, 0, -1)
    ring += [up, down]
    up, down, first_low, first_high = lax.optimization_barrier((up, down, first_low, first_high))
    ring.append(jnp.concatenate([move(up[:16], 0, 1), move(down[16:], 0, -1)], axis=0))
    last = jnp.stack(ring)
    last_left, last_right = move(last, 1, 0), move(last, -1, 0)
    last_low, last_high = move(last_left[:2], 1, 0), move(last_right[2:], -1, 0)

    steps = jnp.tile(timesteps, 128 // samples).reshape(1, 128)
    out_rows = kernel(
        conv_kernel,
        shape(slots, cells),
        (),
        (act_all, weight, maps, time_table.reshape(-1, packed), steps, pick),
        "conv",
        vmem_mib=24,
        after=(6, dout_left),
    )
    grad_rows, stats = kernel(
        backward_kernel,
        (shape(slots, cells), shape(16, chan, dtype=F32)),
        (),
        (*dacts, maps, dout, gain, bias, pick),
        "norm_backward",
    )

    stats = stats.reshape(2, 8, chan)[:, 0].reshape(1, 2 * chan)
    upper = stats.astype(BF16)
    lower = (stats - upper.astype(F32)).astype(BF16)
    extra = jnp.concatenate([upper, lower], axis=1).reshape(1, 1, 1, packed)
    extra = jnp.broadcast_to(extra, (dp_count, 1, height, packed))
    payload = jnp.concatenate(
        [
            out_rows.reshape(dp_count, cap, height, packed),
            grad_rows.reshape(dp_count, cap, height, packed),
            extra,
        ],
        axis=1,
    )
    back = lax.all_to_all(payload, "dp", split_axis=0, concat_axis=0, tiled=True)
    out_slots = back[:, :cap].reshape(slots, height, 1, packed)
    grad_slots = back[:, cap : 2 * cap].reshape(slots, height, 1, packed)
    sent = jnp.sum(back[:, 2 * cap, 0, :].astype(F32), axis=0)
    grad_norm = (sent[: 2 * chan] + sent[2 * chan :]).reshape(2, chan) * scale

    width = 256
    sources = (
        first, last, first_left, last_left, first_right, last_right, first_low, first_high, last_low, last_high
    )
    grad_weight = pl.pallas_call(
        functools.partial(finish_kernel, scale),
        grid=(pl.cdiv(wide, width),),
        in_specs=[smem, smem]
        + [pl.BlockSpec((ref.shape[0], piece, width), lambda i: (0, 0, i)) for ref in sources],
        out_specs=pl.BlockSpec((width, C), lambda i: (i, 0)),
        out_shape=jax.ShapeDtypeStruct((wide, C), F32),
        scratch_shapes=[pltpu.VMEM((C // NX, width), F32), pltpu.VMEM((256, width), F32)],
        name="grad_weight_out",
        compiler_params=pltpu.CompilerParams(vmem_limit_bytes=40 * 1024 * 1024),
    )(x_ring, z_ring, *sources)
    return (out_slots, grad_slots, grad_weight.reshape(3, 3, chan, C), grad_norm)


def solution(mesh):
    in_specs = (
        P("dp", None, "chan", None),
        P("dp", None),
        P("dp"),
        P(None, "chan", None),
        P("chan"),
        P("chan"),
        P(None, None, "chan", None),
        P("dp", None, "chan", None),
    )
    out_specs = (
        P("dp", None, "chan", None),
        P("dp", None, "chan", None),
        P(None, None, "chan", None),
        P(None, "chan"),
    )
    return jax.shard_map(
        per_device, mesh=mesh, in_specs=in_specs, out_specs=out_specs, check_vma=False
    )
```

```python
import functools
import math

import jax
import jax.numpy as jnp
from jax import lax
from jax.experimental import pallas as pl
from jax.experimental.pallas import tpu as pltpu
from jax.sharding import PartitionSpec as P

C = 1280
GROUPS = 32
SIDE = 4
CELLS = 16
EPS = 1e-05
NX = 4
NZ = 8
F32 = jnp.float32
BF16 = jnp.bfloat16
NT = (((1,), (1,)), ((), ()))
TN = (((0,), (0,)), ((), ()))


def lane_block(shape):
    return (lax.broadcasted_iota(jnp.int32, shape, 1) // 32) % SIDE


def to_columns(rows, pick, chan):
    wide = lax.dot_general(rows, pick, TN, preferred_element_type=F32)
    block = lane_block((chan, 128))
    parts = []
    for h in range(SIDE):
        got = jnp.zeros((chan, 128), F32)
        for w in range(SIDE):
            start = (h * SIDE + w) * chan
            got = jnp.where(block == w, wide[start : start + chan, :], got)
        parts.append(got)
    return jnp.concatenate(parts, axis=1)


def to_rows(columns, pick):
    chan = columns.shape[0]
    block = lane_block((chan, 128))
    parts = []
    for h in range(SIDE):
        here = columns[:, 128 * h : 128 * h + 128]
        masked = [jnp.where(block == w, here, 0.0) for w in range(SIDE)]
        stack = jnp.concatenate(masked, axis=0).astype(BF16)
        parts.append(lax.dot_general(pick, stack, NT, preferred_element_type=F32))
    return jnp.concatenate(parts, axis=1)


def group_mean(values):
    chan, lanes = values.shape
    size = C // GROUPS
    spread = []
    for g in range(chan // size):
        total = jnp.sum(values[g * size : (g + 1) * size, :], axis=0, keepdims=True)
        folded = total[:, 0:128] + total[:, 128:256] + total[:, 256:384] + total[:, 384:512]
        folded = jnp.broadcast_to(folded, (8, 128))
        folded = folded + pltpu.roll(folded, 64, 1)
        folded = folded + pltpu.roll(folded, 32, 1)
        mean = folded[0:1, :] * (1.0 / (size * CELLS))
        wide = jnp.concatenate([mean] * SIDE, axis=1)
        spread.append(jnp.broadcast_to(wide, (size, lanes)))
    return jnp.concatenate(spread, axis=0)


def normalise(values):
    center = values - group_mean(values)
    inverse = lax.rsqrt(group_mean(center * center) + EPS)
    return center * inverse, inverse


def shift_rows(values, step):
    zero = jnp.zeros((values.shape[0], 128), values.dtype)
    if step == 0:
        return values
    if step > 0:
        return jnp.concatenate([values[:, 128:], zero], axis=1)
    return jnp.concatenate([zero, values[:, :-128]], axis=1)


def shift_columns(values, step):
    if step == 0:
        return values
    lanes = values.shape[1]
    block = lane_block(values.shape)
    moved = pltpu.roll(values, (-32 * step) % lanes, 1)
    return jnp.where((block + step >= 0) & (block + step < SIDE), moved, 0.0)


def im2col(dout, store):
    for col in range(3):
        moved = shift_columns(dout, -(col - 1)).astype(BF16)
        for row in range(3):
            store(row * 3 + col, shift_rows(moved, -(row - 1)))


def column(row):
    n = row.shape[1]
    eye = lax.broadcasted_iota(jnp.int32, (n, n), 0) == lax.broadcasted_iota(jnp.int32, (n, n), 1)
    return jnp.sum(jnp.where(eye, jnp.broadcast_to(row, (n, n)), 0.0), axis=1, keepdims=True)


def forward_kernel(rows_ref, pick_ref, gain_ref, bias_ref, maps_ref, act_ref):
    chan = act_ref.shape[0]
    maps = to_columns(rows_ref[...], pick_ref[...], chan)
    normed, _ = normalise(maps)
    shifted = normed * column(gain_ref[...]) + column(bias_ref[...])
    maps_ref[...] = maps.astype(BF16)
    act_ref[...] = (shifted * jax.nn.sigmoid(shifted)).astype(BF16)


def forward_conv_kernel(
    where_ref, own_ref, a_ref, b_ref, c_ref, other_ref, weight_ref, maps_ref, table_ref, steps_ref, pick_ref,
    slices_ref, out_ref, all_ref,
):
    chan = own_ref.shape[0]

    def put(block, value):
        all_ref[pl.ds(pl.multiple_of(block * chan, 32), chan), :] = value

    for j, ref in enumerate((own_ref, a_ref, b_ref, c_ref)):
        put(where_ref[j], ref[...])
        put(where_ref[4 + j], other_ref[j])
    for x in range(NX):
        slices_ref[x, 0:256, :] = all_ref[256 * x : 256 * x + 256, :]
        slices_ref[x, 256:320, :] = all_ref[1024 + 64 * x : 1088 + 64 * x, :]
    conv = None
    for col in range(3):
        column_sum = None
        for row in range(3):
            tap = row * 3 + col
            term = jnp.dot(
                weight_ref[tap * chan : (tap + 1) * chan, :], all_ref[...], preferred_element_type=F32
            )
            term = shift_rows(term, row - 1)
            column_sum = term if column_sum is None else column_sum + term
        column_sum = shift_columns(column_sum, col - 1)
        conv = column_sum if conv is None else conv + column_sum
    rows = table_ref.shape[0]
    steps = steps_ref[...]
    hot = lax.broadcasted_iota(jnp.int32, (rows, 128), 0) == steps // SIDE
    wide = lax.dot_general(table_ref[...], hot.astype(BF16), TN, preferred_element_type=F32)
    embed = jnp.zeros((chan, 128), F32)
    for j in range(SIDE):
        embed = jnp.where(steps % SIDE == j, wide[j * chan : (j + 1) * chan, :], embed)
    embed = jnp.concatenate([embed] * SIDE, axis=1)
    out = maps_ref[...].astype(F32) + conv + embed
    out_ref[...] = to_rows(out, pick_ref[...]).astype(BF16)


def pick_kernel(rows_ref, pick_ref, dout_ref):
    dout_ref[...] = to_columns(rows_ref[...], pick_ref[...], dout_ref.shape[0]).astype(BF16)


def add_kernel(keep_ref, got_ref, *out_refs):
    for j, ref in enumerate(out_refs):
        ref[...] = keep_ref[j] + got_ref[j]


def grad_kernel(where_ref, x_ref, z_ref, act_ref, weight_ref, *refs):
    douts, outs = refs[:NX], refs[NX : NX + NZ]
    keep_ref, give_ref, wide_ref, total_ref, full_ref = refs[NX + NZ :]
    chan = douts[0].shape[0]
    total = None
    for k in range(NX):

        def store(tap, rows):
            wide_ref[k, tap * chan : (tap + 1) * chan, :] = rows

        im2col(douts[k][...].astype(F32), store)
        part = lax.dot_general(act_ref[x_ref[k]], wide_ref[k], NT, preferred_element_type=F32)
        total = part if total is None else total + part
    total_ref[...] = total
    size = outs[0].shape[0]
    for k in range(NZ):
        start = pl.multiple_of(z_ref[k] * size, 8)
        outs[k][...] = total_ref[pl.ds(start, size), :].astype(outs[k].dtype)
    full_ref[...] = lax.dot_general(weight_ref[...], wide_ref[0], TN, preferred_element_type=F32)
    for j in range(4):
        keep_ref[j] = full_ref[pl.ds(pl.multiple_of(where_ref[j] * chan, 32), chan), :]
        give_ref[j] = full_ref[pl.ds(pl.multiple_of(where_ref[4 + j] * chan, 32), chan), :]


def sum_kernel(_, own_ref, *refs):
    total = own_ref[...]
    for ref in refs[:-1]:
        total = total + ref[...].astype(F32)
    refs[-1][...] = total.astype(BF16)


def backward_kernel(
    own_ref, a_ref, b_ref, c_ref, maps_ref, dout_ref, gain_ref, bias_ref, pick_ref, _, grad_ref, sums_ref
):
    gain = column(gain_ref[...])
    dact = own_ref[...] + a_ref[...] + b_ref[...] + c_ref[...]
    normed, inverse = normalise(maps_ref[...].astype(F32))
    shifted = normed * gain + column(bias_ref[...])
    gate = jax.nn.sigmoid(shifted)
    dshift = dact * gate * (1.0 + shifted * (1.0 - gate))
    ones = jnp.ones((8, dshift.shape[1]), F32)
    exact = lax.Precision.HIGHEST
    sums_ref[0:8, :] = lax.dot_general(ones, dshift * normed, NT, precision=exact, preferred_element_type=F32)
    sums_ref[8:16, :] = lax.dot_general(ones, dshift, NT, precision=exact, preferred_element_type=F32)
    dnormed = dshift * gain
    dmaps = inverse * (dnormed - group_mean(dnormed) - normed * group_mean(dnormed * normed))
    grad_ref[...] = to_rows(dout_ref[...].astype(F32) + dmaps, pick_ref[...]).astype(BF16)


def place_z_kernel(z_ref, *refs):
    out_ref = refs[-1]
    for k in range(7):
        out_ref[z_ref[k]] = refs[k][...]
    out_ref[z_ref[7]] = jnp.concatenate([refs[7][...], refs[8][...]], axis=0)


def finish_kernel(scale, x_ref, own_ref, left_ref, right_ref, low_ref, high_ref, out_ref, tail_ref):
    def flat(ref):
        value = ref[...].astype(F32)
        return value.reshape(value.shape[0] * value.shape[1], value.shape[2])

    pieces = [flat(own_ref), flat(left_ref), flat(right_ref), jnp.concatenate([flat(low_ref), flat(high_ref)], axis=0)]
    for k, piece in enumerate(pieces):
        out_ref[:, pl.ds(pl.multiple_of(x_ref[k] * 256, 256), 256)] = piece[0:256].T * scale
        tail_ref[pl.ds(pl.multiple_of(x_ref[k] * 64, 64), 64), :] = piece[256:320]
    out_ref[:, 1024:1280] = tail_ref[...].T * scale


def per_device(
    latents, bucket_ids, timesteps, time_table, norm_gain, norm_bias, conv_weight, cotangent
):
    dp_count = lax.axis_size("dp")
    samples, height, _, packed = latents.shape
    chan = packed // SIDE
    slots = cotangent.shape[0]
    cap = slots // dp_count
    cells = height * packed
    lanes = samples * CELLS
    wide = 9 * chan
    piece = C // NX // NZ
    scale = 1.0 / math.sqrt(samples * dp_count * CELLS)
    place = lax.axis_index("dp")
    x, z = place // NZ, place % NZ
    mine_chan = lax.axis_index("chan")
    y, core = mine_chan // 2, mine_chan % 2
    vmem = pl.BlockSpec(memory_space=pltpu.VMEM)
    smem = pl.BlockSpec(memory_space=pltpu.SMEM)
    anywhere = pl.BlockSpec(memory_space=pl.ANY)

    def move(value, dx, dz):
        pairs = [
            (i * NZ + j, (i + dx) % NX * NZ + (j + dz) % NZ) for i in range(NX) for j in range(NZ)
        ]
        return lax.ppermute(value, "dp", pairs)

    def move_chan(value, dy, flip):
        pairs = [(i * 2 + j, (i + dy) % 4 * 2 + (j ^ flip)) for i in range(4) for j in range(2)]
        return lax.ppermute(value, "chan", pairs)

    def kernel(body, out_shape, scalars, operands, name, scratch=(), vmem_mib=12, after=None):
        specs = [smem] * len(scalars) + [vmem] * len(operands)
        operands = list(operands)
        if after is not None:
            specs.insert(len(scalars) + after[0], anywhere)
            operands.insert(after[0], after[1])
        return pl.pallas_call(
            body,
            in_specs=specs,
            out_shape=out_shape,
            scratch_shapes=list(scratch),
            name=name,
            compiler_params=pltpu.CompilerParams(vmem_limit_bytes=vmem_mib * 1024 * 1024),
            cost_estimate=pl.CostEstimate(flops=1000, bytes_accessed=1000, transcendentals=0),
        )(*scalars, *operands)

    def shape(*dims, dtype=BF16):
        return jax.ShapeDtypeStruct(dims, dtype)

    steps_y = jnp.array([0, 1, 3, 2], jnp.int32)
    to_y = (y + steps_y) % 4 * 2
    from_y = (y - steps_y) % 4 * 2
    give_where = jnp.concatenate([to_y + core, to_y + 1 - core])
    act_where = jnp.concatenate([from_y + core, from_y + 1 - core])
    x_from = (x - jnp.arange(NX, dtype=jnp.int32)) % NX
    along_x = [[j + NZ * i for i in range(NX)] for j in range(NZ)]
    z_to = (z + jnp.arange(NZ, dtype=jnp.int32)) % NZ
    z_ring = (z + jnp.array([0, -1, 1, -2, 2, -3, 3, 4], jnp.int32)) % NZ
    x_ring = (x + jnp.array([0, -1, 1, 2], jnp.int32)) % NX

    gain = norm_gain.reshape(1, chan)
    bias = norm_bias.reshape(1, chan)
    weight = conv_weight.reshape(wide, C)

    same = (
        lax.broadcasted_iota(jnp.int32, (samples, 128), 0)
        == lax.broadcasted_iota(jnp.int32, (samples, 128), 1) % samples
    ).astype(BF16)
    maps, act = kernel(
        forward_kernel,
        (shape(chan, lanes), shape(chan, lanes)),
        (),
        (latents.reshape(samples, cells), same, gain, bias),
        "norm_forward",
    )
    near = [move_chan(act, 1, 0), move_chan(act, -1, 0), move_chan(act, 2, 0)]
    other = move_chan(jnp.stack([act] + near), 0, 1)
    buckets = bucket_ids[:, 0]
    order = jnp.arange(samples, dtype=jnp.int32)
    earlier = (buckets[:, None] == buckets[None, :]) & (order[None, :] < order[:, None])
    target = buckets * cap + jnp.sum(earlier.astype(jnp.int32), axis=1)
    target = jnp.tile(target, 128 // samples)
    pick = (target[None, :] == jnp.arange(slots, dtype=jnp.int32)[:, None]).astype(BF16)

    steps = jnp.tile(timesteps, 128 // samples).reshape(1, 128)
    act_slices, out_rows = kernel(
        forward_conv_kernel,
        (shape(NX, C // NX, lanes), shape(slots, cells)),
        (act_where,),
        (act, *near, other, weight, maps, time_table.reshape(-1, packed), steps, pick),
        "forward_conv",
        scratch=[pltpu.VMEM((C, lanes), BF16)],
        vmem_mib=24,
    )
    act_x = lax.all_to_all(
        act_slices, "dp", split_axis=0, concat_axis=0, tiled=True, axis_index_groups=along_x
    )

    got = lax.all_to_all(cotangent, "dp", split_axis=0, concat_axis=0, tiled=True)
    dout = kernel(
        pick_kernel,
        shape(chan, lanes),
        (),
        (got.reshape(slots, cells), pick),
        "pick_dout",
    )
    douts = [dout] + [move(dout, k, 0) for k in range(1, NX)]

    *chunks, keep, give = kernel(
        grad_kernel,
        (shape(piece, wide, dtype=F32),)
        + (shape(piece, wide),) * (NZ - 1)
        + (shape(4, chan, lanes, dtype=F32),) * 2,
        (give_where, x_from, z_to),
        (act_x, weight, *douts),
        "grad_weight",
        scratch=[
            pltpu.VMEM((NX, wide, lanes), BF16),
            pltpu.VMEM((C // NX, wide), F32),
            pltpu.VMEM((C, lanes), F32),
        ],
        vmem_mib=32,
    )
    came = [move(chunks[k], 0, k) for k in range(1, NZ)]
    sums = kernel(
        add_kernel,
        (shape(chan, lanes, dtype=F32),) * 4,
        (),
        (keep, move_chan(give, 0, 1)),
        "add_cores",
    )
    dacts = [sums[0], move_chan(sums[1], 1, 0), move_chan(sums[2], -1, 0), move_chan(sums[3], 2, 0)]
    mine = kernel(
        sum_kernel, shape(piece, wide), (), (chunks[0], *came), "sum_z", after=(0, sums[0])
    )
    up = down = mine
    ring = [mine]
    for _ in range(3):
        up, down = move(up, 0, 1), move(down, 0, -1)
        ring += [up, down]
    ring += [move(up[:16], 0, 1), move(down[16:], 0, -1)]
    block = kernel(place_z_kernel, shape(NZ, piece, wide), (z_ring,), tuple(ring), "place_z")
    left, right = move(block, 1, 0), move(block, -1, 0)
    half = NZ // 2
    low, high = move(left[:half], 1, 0), move(right[half:], -1, 0)

    grad_rows, stats = kernel(
        backward_kernel,
        (shape(slots, cells), shape(16, chan, dtype=F32)),
        (),
        (*dacts, maps, dout, gain, bias, pick),
        "norm_backward",
        after=(9, block),
    )

    stats = stats.reshape(2, 8, chan)[:, 0].reshape(1, 2 * chan)
    upper = stats.astype(BF16)
    lower = (stats - upper.astype(F32)).astype(BF16)
    extra = jnp.concatenate([upper, lower], axis=1).reshape(1, 1, 1, packed)
    extra = jnp.broadcast_to(extra, (dp_count, 1, height, packed))
    payload = jnp.concatenate(
        [
            out_rows.reshape(dp_count, cap, height, packed),
            grad_rows.reshape(dp_count, cap, height, packed),
            extra,
        ],
        axis=1,
    )
    back = lax.all_to_all(payload, "dp", split_axis=0, concat_axis=0, tiled=True)
    out_slots = back[:, :cap].reshape(slots, height, 1, packed)
    grad_slots = back[:, cap : 2 * cap].reshape(slots, height, 1, packed)
    sent = jnp.sum(back[:, 2 * cap, 0, :].astype(F32), axis=0)
    grad_norm = (sent[: 2 * chan] + sent[2 * chan :]).reshape(2, chan) * scale

    width = 256
    full = pl.BlockSpec((NZ, piece, width), lambda i: (0, 0, i))
    part = pl.BlockSpec((half, piece, width), lambda i: (0, 0, i))
    grad_weight = pl.pallas_call(
        functools.partial(finish_kernel, scale),
        grid=(pl.cdiv(wide, width),),
        in_specs=[smem, full, full, full, part, part],
        out_specs=pl.BlockSpec((width, C), lambda i: (i, 0)),
        out_shape=jax.ShapeDtypeStruct((wide, C), F32),
        scratch_shapes=[pltpu.VMEM((256, width), F32)],
        name="grad_weight_out",
        compiler_params=pltpu.CompilerParams(vmem_limit_bytes=40 * 1024 * 1024),
    )(x_ring, block, left, right, low, high)
    return (out_slots, grad_slots, grad_weight.reshape(3, 3, chan, C), grad_norm)


def solution(mesh):
    in_specs = (
        P("dp", None, "chan", None),
        P("dp", None),
        P("dp"),
        P(None, "chan", None),
        P("chan"),
        P("chan"),
        P(None, None, "chan", None),
        P("dp", None, "chan", None),
    )
    out_specs = (
        P("dp", None, "chan", None),
        P("dp", None, "chan", None),
        P(None, None, "chan", None),
        P(None, "chan"),
    )
    return jax.shard_map(
        per_device, mesh=mesh, in_specs=in_specs, out_specs=out_specs, check_vma=False
    )
```

```python
import functools
import math

import jax
import jax.numpy as jnp
from jax import lax
from jax.experimental import pallas as pl
from jax.experimental.pallas import tpu as pltpu
from jax.sharding import PartitionSpec as P

C = 1280
GROUPS = 32
SIDE = 4
CELLS = 16
EPS = 1e-05
NX = 4
NZ = 8
F32 = jnp.float32
BF16 = jnp.bfloat16
NT = (((1,), (1,)), ((), ()))
TN = (((0,), (0,)), ((), ()))


def lane_block(shape):
    return (lax.broadcasted_iota(jnp.int32, shape, 1) // 32) % SIDE


def to_columns(rows, pick, chan):
    wide = lax.dot_general(rows, pick, TN, preferred_element_type=F32)
    block = lane_block((chan, 128))
    parts = []
    for h in range(SIDE):
        got = jnp.zeros((chan, 128), F32)
        for w in range(SIDE):
            start = (h * SIDE + w) * chan
            got = jnp.where(block == w, wide[start : start + chan, :], got)
        parts.append(got)
    return jnp.concatenate(parts, axis=1)


def to_rows(columns, pick):
    chan = columns.shape[0]
    block = lane_block((chan, 128))
    parts = []
    for h in range(SIDE):
        here = columns[:, 128 * h : 128 * h + 128]
        masked = [jnp.where(block == w, here, 0.0) for w in range(SIDE)]
        stack = jnp.concatenate(masked, axis=0).astype(BF16)
        parts.append(lax.dot_general(pick, stack, NT, preferred_element_type=F32))
    return jnp.concatenate(parts, axis=1)


def group_mean(values):
    chan, lanes = values.shape
    size = C // GROUPS
    spread = []
    for g in range(chan // size):
        total = jnp.sum(values[g * size : (g + 1) * size, :], axis=0, keepdims=True)
        folded = total[:, 0:128] + total[:, 128:256] + total[:, 256:384] + total[:, 384:512]
        folded = jnp.broadcast_to(folded, (8, 128))
        folded = folded + pltpu.roll(folded, 64, 1)
        folded = folded + pltpu.roll(folded, 32, 1)
        mean = folded[0:1, :] * (1.0 / (size * CELLS))
        wide = jnp.concatenate([mean] * SIDE, axis=1)
        spread.append(jnp.broadcast_to(wide, (size, lanes)))
    return jnp.concatenate(spread, axis=0)


def normalise(values):
    center = values - group_mean(values)
    inverse = lax.rsqrt(group_mean(center * center) + EPS)
    return center * inverse, inverse


def shift_rows(values, step):
    zero = jnp.zeros((values.shape[0], 128), values.dtype)
    if step == 0:
        return values
    if step > 0:
        return jnp.concatenate([values[:, 128:], zero], axis=1)
    return jnp.concatenate([zero, values[:, :-128]], axis=1)


def shift_columns(values, step):
    if step == 0:
        return values
    lanes = values.shape[1]
    block = lane_block(values.shape)
    moved = pltpu.roll(values, (-32 * step) % lanes, 1)
    return jnp.where((block + step >= 0) & (block + step < SIDE), moved, 0.0)


def im2col(dout, store):
    for col in range(3):
        moved = shift_columns(dout, -(col - 1)).astype(BF16)
        for row in range(3):
            store(row * 3 + col, shift_rows(moved, -(row - 1)))


def column(row):
    n = row.shape[1]
    eye = lax.broadcasted_iota(jnp.int32, (n, n), 0) == lax.broadcasted_iota(jnp.int32, (n, n), 1)
    return jnp.sum(jnp.where(eye, jnp.broadcast_to(row, (n, n)), 0.0), axis=1, keepdims=True)


def forward_kernel(rows_ref, pick_ref, gain_ref, bias_ref, maps_ref, act_ref):
    chan = act_ref.shape[0]
    maps = to_columns(rows_ref[...], pick_ref[...], chan)
    normed, _ = normalise(maps)
    shifted = normed * column(gain_ref[...]) + column(bias_ref[...])
    maps_ref[...] = maps.astype(BF16)
    act_ref[...] = (shifted * jax.nn.sigmoid(shifted)).astype(BF16)


def place_act_kernel(where_ref, core_ref, own_ref, a_ref, b_ref, c_ref, other_ref, half_ref, all_ref):
    chan = own_ref.shape[0]

    def put(block, value):
        all_ref[pl.ds(pl.multiple_of(block * chan, 32), chan), :] = value

    for j, ref in enumerate((own_ref, a_ref, b_ref, c_ref)):
        put(where_ref[j], ref[...])
        put(where_ref[4 + j], other_ref[j])
    for core in range(2):

        @pl.when(core_ref[0] == core)
        def _():
            for x in range(NX):
                if core == 0:
                    half_ref[x] = all_ref[256 * x : 256 * x + 160, :]
                else:
                    half_ref[x, 0:96, :] = all_ref[256 * x + 160 : 256 * x + 256, :]
                    half_ref[x, 96:160, :] = all_ref[1024 + 64 * x : 1088 + 64 * x, :]


def forward_conv_kernel(all_ref, weight_ref, maps_ref, table_ref, steps_ref, pick_ref, _, out_ref):
    chan = maps_ref.shape[0]
    conv = None
    for col in range(3):
        column_sum = None
        for row in range(3):
            tap = row * 3 + col
            term = jnp.dot(
                weight_ref[tap * chan : (tap + 1) * chan, :], all_ref[...], preferred_element_type=F32
            )
            term = shift_rows(term, row - 1)
            column_sum = term if column_sum is None else column_sum + term
        column_sum = shift_columns(column_sum, col - 1)
        conv = column_sum if conv is None else conv + column_sum
    rows = table_ref.shape[0]
    steps = steps_ref[...]
    hot = lax.broadcasted_iota(jnp.int32, (rows, 128), 0) == steps // SIDE
    wide = lax.dot_general(table_ref[...], hot.astype(BF16), TN, preferred_element_type=F32)
    embed = jnp.zeros((chan, 128), F32)
    for j in range(SIDE):
        embed = jnp.where(steps % SIDE == j, wide[j * chan : (j + 1) * chan, :], embed)
    embed = jnp.concatenate([embed] * SIDE, axis=1)
    out = maps_ref[...].astype(F32) + conv + embed
    out_ref[...] = to_rows(out, pick_ref[...]).astype(BF16)


def pick_kernel(rows_ref, pick_ref, half_ref, dout_ref, send_ref):
    chan = dout_ref.shape[0]
    dout = to_columns(rows_ref[...], pick_ref[...], chan).astype(BF16)
    dout_ref[...] = dout
    for x in range(NX):
        send_ref[x, 0:chan, :] = half_ref[x]
        send_ref[x, chan : 2 * chan, :] = dout


def add_kernel(keep_ref, got_ref, *out_refs):
    for j, ref in enumerate(out_refs):
        ref[...] = keep_ref[j] + got_ref[j]


def grad_kernel(where_ref, core_ref, x_ref, got_ref, other_ref, weight_ref, out_ref, keep_ref, give_ref, *scratch):
    held_ref, act_ref, wide_ref, full_ref, sem = scratch
    fetch = pltpu.make_async_copy(weight_ref, held_ref, sem)
    fetch.start()
    chan = other_ref.shape[1]
    mine = pl.multiple_of(core_ref[0] * chan, 32)
    rest = pl.multiple_of((1 - core_ref[0]) * chan, 32)
    total = None
    for x in range(NX):

        def store(tap, rows):
            wide_ref[x, tap * chan : (tap + 1) * chan, :] = rows

        im2col(got_ref[x, chan : 2 * chan, :].astype(F32), store)
        act_ref[x, pl.ds(mine, chan), :] = got_ref[x, 0:chan, :]
        act_ref[x, pl.ds(rest, chan), :] = other_ref[x]
        part = lax.dot_general(act_ref[x], wide_ref[x], NT, preferred_element_type=F32)
        total = part if total is None else total + part
    out_ref[...] = total.astype(BF16)
    fetch.wait()
    full_ref[...] = lax.dot_general(held_ref[...], wide_ref[x_ref[0]], TN, preferred_element_type=F32)
    for j in range(4):
        keep_ref[j] = full_ref[pl.ds(pl.multiple_of(where_ref[j] * chan, 32), chan), :]
        give_ref[j] = full_ref[pl.ds(pl.multiple_of(where_ref[4 + j] * chan, 32), chan), :]


def sum_kernel(_a, _b, _c, parts_ref, out_ref):
    total = parts_ref[0].astype(F32)
    for k in range(1, NZ):
        total = total + parts_ref[k].astype(F32)
    out_ref[...] = total.astype(BF16)


def backward_kernel(
    own_ref, a_ref, b_ref, c_ref, maps_ref, dout_ref, gain_ref, bias_ref, pick_ref, grad_ref, sums_ref
):
    gain = column(gain_ref[...])
    dact = own_ref[...] + a_ref[...] + b_ref[...] + c_ref[...]
    normed, inverse = normalise(maps_ref[...].astype(F32))
    shifted = normed * gain + column(bias_ref[...])
    gate = jax.nn.sigmoid(shifted)
    dshift = dact * gate * (1.0 + shifted * (1.0 - gate))
    ones = jnp.ones((8, dshift.shape[1]), F32)
    exact = lax.Precision.HIGHEST
    sums_ref[0:8, :] = lax.dot_general(ones, dshift * normed, NT, precision=exact, preferred_element_type=F32)
    sums_ref[8:16, :] = lax.dot_general(ones, dshift, NT, precision=exact, preferred_element_type=F32)
    dnormed = dshift * gain
    dmaps = inverse * (dnormed - group_mean(dnormed) - normed * group_mean(dnormed * normed))
    grad_ref[...] = to_rows(dout_ref[...].astype(F32) + dmaps, pick_ref[...]).astype(BF16)


def finish_kernel(scale, x_ref, *refs):
    halves, (out_ref, tail_ref) = refs[:-2], refs[-2:]

    for k in range(NX):
        piece = jnp.concatenate([halves[2 * k][...].astype(F32), halves[2 * k + 1][...].astype(F32)], axis=0)
        out_ref[:, pl.ds(pl.multiple_of(x_ref[k] * 256, 256), 256)] = piece[0:256].T * scale
        tail_ref[pl.ds(pl.multiple_of(x_ref[k] * 64, 64), 64), :] = piece[256:320]
    out_ref[:, 1024:1280] = tail_ref[...].T * scale


def per_device(
    latents, bucket_ids, timesteps, time_table, norm_gain, norm_bias, conv_weight, cotangent
):
    dp_count = lax.axis_size("dp")
    samples, height, _, packed = latents.shape
    chan = packed // SIDE
    slots = cotangent.shape[0]
    cap = slots // dp_count
    cells = height * packed
    lanes = samples * CELLS
    wide = 9 * chan
    piece = C // NX // NZ
    scale = 1.0 / math.sqrt(samples * dp_count * CELLS)
    place = lax.axis_index("dp")
    x = place // NZ
    mine_chan = lax.axis_index("chan")
    y, core = mine_chan // 2, mine_chan % 2
    vmem = pl.BlockSpec(memory_space=pltpu.VMEM)
    smem = pl.BlockSpec(memory_space=pltpu.SMEM)
    anywhere = pl.BlockSpec(memory_space=pl.ANY)

    def move(value, dx, dz):
        pairs = [
            (i * NZ + j, (i + dx) % NX * NZ + (j + dz) % NZ) for i in range(NX) for j in range(NZ)
        ]
        return lax.ppermute(value, "dp", pairs)

    def move_chan(value, dy, flip):
        pairs = [(i * 2 + j, (i + dy) % 4 * 2 + (j ^ flip)) for i in range(4) for j in range(2)]
        return lax.ppermute(value, "chan", pairs)

    def kernel(body, out_shape, scalars, operands, name, scratch=(), vmem_mib=12, after=None):
        specs = [smem] * len(scalars) + [vmem] * len(operands)
        operands = list(operands)
        if after is not None:
            at, *extra = after
            specs[len(scalars) + at : len(scalars) + at] = [anywhere] * len(extra)
            operands[at:at] = extra
        return pl.pallas_call(
            body,
            in_specs=specs,
            out_shape=out_shape,
            scratch_shapes=list(scratch),
            name=name,
            compiler_params=pltpu.CompilerParams(vmem_limit_bytes=vmem_mib * 1024 * 1024),
            cost_estimate=pl.CostEstimate(flops=1000, bytes_accessed=1000, transcendentals=0),
        )(*scalars, *operands)

    def shape(*dims, dtype=BF16):
        return jax.ShapeDtypeStruct(dims, dtype)

    steps_y = jnp.array([0, 1, 3, 2], jnp.int32)
    to_y = (y + steps_y) % 4 * 2
    from_y = (y - steps_y) % 4 * 2
    give_where = jnp.concatenate([to_y + core, to_y + 1 - core])
    act_where = jnp.concatenate([from_y + core, from_y + 1 - core])
    core_at = core.reshape(1)
    along_z = [[j + NZ * i for j in range(NZ)] for i in range(NX)]
    along_x = [[j + NZ * i for i in range(NX)] for j in range(NZ)]
    x_ring = (x + jnp.array([0, -1, 1, 2], jnp.int32)) % NX

    gain = norm_gain.reshape(1, chan)
    bias = norm_bias.reshape(1, chan)
    weight = conv_weight.reshape(wide, C)

    same = (
        lax.broadcasted_iota(jnp.int32, (samples, 128), 0)
        == lax.broadcasted_iota(jnp.int32, (samples, 128), 1) % samples
    ).astype(BF16)
    maps, act = kernel(
        forward_kernel,
        (shape(chan, lanes), shape(chan, lanes)),
        (),
        (latents.reshape(samples, cells), same, gain, bias),
        "norm_forward",
    )
    near = [move_chan(act, 1, 0), move_chan(act, -1, 0), move_chan(act, 2, 0)]
    other = move_chan(jnp.stack([act] + near), 0, 1)
    buckets = bucket_ids[:, 0]
    order = jnp.arange(samples, dtype=jnp.int32)
    earlier = (buckets[:, None] == buckets[None, :]) & (order[None, :] < order[:, None])
    target = buckets * cap + jnp.sum(earlier.astype(jnp.int32), axis=1)
    target = jnp.tile(target, 128 // samples)
    pick = (target[None, :] == jnp.arange(slots, dtype=jnp.int32)[:, None]).astype(BF16)

    steps = jnp.tile(timesteps, 128 // samples).reshape(1, 128)
    act_half, act_all = kernel(
        place_act_kernel,
        (shape(NX, C // NX // 2, lanes), shape(C, lanes)),
        (act_where, core_at),
        (act, *near, other),
        "place_act",
    )
    got = lax.all_to_all(cotangent, "dp", split_axis=0, concat_axis=0, tiled=True)
    dout, send = kernel(
        pick_kernel,
        (shape(chan, lanes), shape(NX, 2 * chan, lanes)),
        (),
        (got.reshape(slots, cells), pick, act_half),
        "pick_dout",
    )
    got_x = lax.all_to_all(
        send, "dp", split_axis=0, concat_axis=0, tiled=True, axis_index_groups=along_x
    )
    act_other = move_chan(got_x[:, :chan], 0, 1)
    part, keep, give = kernel(
        grad_kernel,
        (shape(C // NX, wide),) + (shape(4, chan, lanes, dtype=F32),) * 2,
        (give_where, core_at, x.reshape(1)),
        (got_x, act_other),
        "grad_weight",
        scratch=[
            pltpu.VMEM((wide, C), BF16),
            pltpu.VMEM((NX, C // NX, lanes), BF16),
            pltpu.VMEM((NX, wide, lanes), BF16),
            pltpu.VMEM((C, lanes), F32),
            pltpu.SemaphoreType.DMA,
        ],
        vmem_mib=36,
        after=(2, weight),
    )
    parts = lax.all_to_all(
        part.reshape(NZ, piece, wide),
        "dp",
        split_axis=0,
        concat_axis=0,
        tiled=True,
        axis_index_groups=along_z,
    )
    sums = kernel(
        add_kernel,
        (shape(chan, lanes, dtype=F32),) * 4,
        (),
        (keep, move_chan(give, 0, 1)),
        "add_cores",
    )
    dacts = [sums[0], move_chan(sums[1], 1, 0), move_chan(sums[2], -1, 0), move_chan(sums[3], 2, 0)]
    out_rows = kernel(
        forward_conv_kernel,
        shape(slots, cells),
        (),
        (act_all, weight, maps, time_table.reshape(-1, packed), steps, pick),
        "forward_conv",
        vmem_mib=24,
        after=(6, sums[0]),
    )
    mine = kernel(sum_kernel, shape(piece, wide), (), (parts,), "sum_z", after=(0, *dacts[1:]))
    block = lax.all_gather(mine, "dp", axis=0, tiled=True, axis_index_groups=along_z)
    half = C // NX // 2
    low, high = block[:half], block[half:]
    left_low, right_high = move(low, 1, 0), move(high, -1, 0)
    left_high, right_low = move(high, 1, 0), move(low, -1, 0)
    far_low, far_high = move(left_low, 1, 0), move(right_high, -1, 0)

    grad_rows, stats = kernel(
        backward_kernel,
        (shape(slots, cells), shape(16, chan, dtype=F32)),
        (),
        (*dacts, maps, dout, gain, bias, pick),
        "norm_backward",
    )

    stats = stats.reshape(2, 8, chan)[:, 0].reshape(1, 2 * chan)
    upper = stats.astype(BF16)
    lower = (stats - upper.astype(F32)).astype(BF16)
    extra = jnp.concatenate([upper, lower], axis=1).reshape(1, 1, 1, packed)
    extra = jnp.broadcast_to(extra, (dp_count, 1, height, packed))
    payload = jnp.concatenate(
        [
            out_rows.reshape(dp_count, cap, height, packed),
            grad_rows.reshape(dp_count, cap, height, packed),
            extra,
        ],
        axis=1,
    )
    back = lax.all_to_all(payload, "dp", split_axis=0, concat_axis=0, tiled=True)
    out_slots = back[:, :cap].reshape(slots, height, 1, packed)
    grad_slots = back[:, cap : 2 * cap].reshape(slots, height, 1, packed)
    sent = jnp.sum(back[:, 2 * cap, 0, :].astype(F32), axis=0)
    grad_norm = (sent[: 2 * chan] + sent[2 * chan :]).reshape(2, chan) * scale

    width = 256
    halves = (low, high, left_low, left_high, right_low, right_high, far_low, far_high)
    grad_weight = pl.pallas_call(
        functools.partial(finish_kernel, scale),
        grid=(pl.cdiv(wide, width),),
        in_specs=[smem] + [pl.BlockSpec((half, width), lambda i: (0, i))] * len(halves),
        out_specs=pl.BlockSpec((width, C), lambda i: (i, 0)),
        out_shape=jax.ShapeDtypeStruct((wide, C), F32),
        scratch_shapes=[pltpu.VMEM((256, width), F32)],
        name="grad_weight_out",
        compiler_params=pltpu.CompilerParams(vmem_limit_bytes=40 * 1024 * 1024),
    )(x_ring, *halves)
    return (out_slots, grad_slots, grad_weight.reshape(3, 3, chan, C), grad_norm)


def solution(mesh):
    in_specs = (
        P("dp", None, "chan", None),
        P("dp", None),
        P("dp"),
        P(None, "chan", None),
        P("chan"),
        P("chan"),
        P(None, None, "chan", None),
        P("dp", None, "chan", None),
    )
    out_specs = (
        P("dp", None, "chan", None),
        P("dp", None, "chan", None),
        P(None, None, "chan", None),
        P(None, "chan"),
    )
    return jax.shard_map(
        per_device, mesh=mesh, in_specs=in_specs, out_specs=out_specs, check_vma=False
    )
```

```python
import functools
import math

import jax
import jax.numpy as jnp
from jax import lax
from jax.experimental import pallas as pl
from jax.experimental.pallas import tpu as pltpu
from jax.sharding import PartitionSpec as P

C = 1280
GROUPS = 32
SIDE = 4
CELLS = 16
EPS = 1e-05
NX = 4
NZ = 8
F32 = jnp.float32
BF16 = jnp.bfloat16
NT = (((1,), (1,)), ((), ()))
TN = (((0,), (0,)), ((), ()))


def lane_block(shape):
    return (lax.broadcasted_iota(jnp.int32, shape, 1) // 32) % SIDE


def to_columns(rows, pick, chan):
    wide = lax.dot_general(rows, pick, TN, preferred_element_type=F32)
    block = lane_block((chan, 128))
    parts = []
    for h in range(SIDE):
        got = jnp.zeros((chan, 128), F32)
        for w in range(SIDE):
            start = (h * SIDE + w) * chan
            got = jnp.where(block == w, wide[start : start + chan, :], got)
        parts.append(got)
    return jnp.concatenate(parts, axis=1)


def to_rows(columns, pick):
    chan = columns.shape[0]
    block = lane_block((chan, 128))
    parts = []
    for h in range(SIDE):
        here = columns[:, 128 * h : 128 * h + 128]
        masked = [jnp.where(block == w, here, 0.0) for w in range(SIDE)]
        stack = jnp.concatenate(masked, axis=0).astype(BF16)
        parts.append(lax.dot_general(pick, stack, NT, preferred_element_type=F32))
    return jnp.concatenate(parts, axis=1)


def group_mean(values):
    chan, lanes = values.shape
    size = C // GROUPS
    spread = []
    for g in range(chan // size):
        total = jnp.sum(values[g * size : (g + 1) * size, :], axis=0, keepdims=True)
        folded = total[:, 0:128] + total[:, 128:256] + total[:, 256:384] + total[:, 384:512]
        folded = jnp.broadcast_to(folded, (8, 128))
        folded = folded + pltpu.roll(folded, 64, 1)
        folded = folded + pltpu.roll(folded, 32, 1)
        mean = folded[0:1, :] * (1.0 / (size * CELLS))
        wide = jnp.concatenate([mean] * SIDE, axis=1)
        spread.append(jnp.broadcast_to(wide, (size, lanes)))
    return jnp.concatenate(spread, axis=0)


def normalise(values):
    center = values - group_mean(values)
    inverse = lax.rsqrt(group_mean(center * center) + EPS)
    return center * inverse, inverse


def shift_rows(values, step):
    zero = jnp.zeros((values.shape[0], 128), values.dtype)
    if step == 0:
        return values
    if step > 0:
        return jnp.concatenate([values[:, 128:], zero], axis=1)
    return jnp.concatenate([zero, values[:, :-128]], axis=1)


def shift_columns(values, step):
    if step == 0:
        return values
    lanes = values.shape[1]
    block = lane_block(values.shape)
    moved = pltpu.roll(values, (-32 * step) % lanes, 1)
    return jnp.where((block + step >= 0) & (block + step < SIDE), moved, 0.0)


def im2col(dout, store):
    for col in range(3):
        moved = shift_columns(dout, -(col - 1)).astype(BF16)
        for row in range(3):
            store(row * 3 + col, shift_rows(moved, -(row - 1)))


def column(row):
    n = row.shape[1]
    eye = lax.broadcasted_iota(jnp.int32, (n, n), 0) == lax.broadcasted_iota(jnp.int32, (n, n), 1)
    return jnp.sum(jnp.where(eye, jnp.broadcast_to(row, (n, n)), 0.0), axis=1, keepdims=True)


def forward_kernel(rows_ref, pick_ref, gain_ref, bias_ref, maps_ref, act_ref):
    chan = act_ref.shape[0]
    maps = to_columns(rows_ref[...], pick_ref[...], chan)
    normed, _ = normalise(maps)
    shifted = normed * column(gain_ref[...]) + column(bias_ref[...])
    maps_ref[...] = maps.astype(BF16)
    act_ref[...] = (shifted * jax.nn.sigmoid(shifted)).astype(BF16)


def place_act_kernel(where_ref, core_ref, own_ref, a_ref, b_ref, c_ref, other_ref, half_ref, all_ref):
    chan = own_ref.shape[0]

    def put(block, value):
        all_ref[pl.ds(pl.multiple_of(block * chan, 32), chan), :] = value

    for j, ref in enumerate((own_ref, a_ref, b_ref, c_ref)):
        put(where_ref[j], ref[...])
        put(where_ref[4 + j], other_ref[j])
    for core in range(2):

        @pl.when(core_ref[0] == core)
        def _():
            for x in range(NX):
                if core == 0:
                    half_ref[x] = all_ref[256 * x : 256 * x + 160, :]
                else:
                    half_ref[x, 0:96, :] = all_ref[256 * x + 160 : 256 * x + 256, :]
                    half_ref[x, 96:160, :] = all_ref[1024 + 64 * x : 1088 + 64 * x, :]


def forward_conv_kernel(all_ref, weight_ref, maps_ref, table_ref, steps_ref, pick_ref, _, out_ref):
    chan = maps_ref.shape[0]
    conv = None
    for col in range(3):
        column_sum = None
        for row in range(3):
            tap = row * 3 + col
            term = jnp.dot(
                weight_ref[tap * chan : (tap + 1) * chan, :], all_ref[...], preferred_element_type=F32
            )
            term = shift_rows(term, row - 1)
            column_sum = term if column_sum is None else column_sum + term
        column_sum = shift_columns(column_sum, col - 1)
        conv = column_sum if conv is None else conv + column_sum
    rows = table_ref.shape[0]
    steps = steps_ref[...]
    hot = lax.broadcasted_iota(jnp.int32, (rows, 128), 0) == steps // SIDE
    wide = lax.dot_general(table_ref[...], hot.astype(BF16), TN, preferred_element_type=F32)
    embed = jnp.zeros((chan, 128), F32)
    for j in range(SIDE):
        embed = jnp.where(steps % SIDE == j, wide[j * chan : (j + 1) * chan, :], embed)
    embed = jnp.concatenate([embed] * SIDE, axis=1)
    out = maps_ref[...].astype(F32) + conv + embed
    out_ref[...] = to_rows(out, pick_ref[...]).astype(BF16)


def pick_kernel(rows_ref, pick_ref, half_ref, dout_ref, send_ref):
    chan = dout_ref.shape[0]
    dout = to_columns(rows_ref[...], pick_ref[...], chan).astype(BF16)
    dout_ref[...] = dout
    for x in range(NX):
        send_ref[x, 0:chan, :] = half_ref[x]
        send_ref[x, chan : 2 * chan, :] = dout


def add_kernel(keep_ref, got_ref, *out_refs):
    for j, ref in enumerate(out_refs):
        ref[...] = keep_ref[j] + got_ref[j]


def grad_kernel(where_ref, core_ref, x_ref, got_ref, other_ref, weight_ref, out_ref, keep_ref, give_ref, *scratch):
    held_ref, act_ref, wide_ref, full_ref, sem = scratch
    fetch = pltpu.make_async_copy(weight_ref, held_ref, sem)
    fetch.start()
    chan = other_ref.shape[1]
    mine = pl.multiple_of(core_ref[0] * chan, 32)
    rest = pl.multiple_of((1 - core_ref[0]) * chan, 32)
    total = None
    for x in range(NX):

        def store(tap, rows):
            wide_ref[x, tap * chan : (tap + 1) * chan, :] = rows

        im2col(got_ref[x, chan : 2 * chan, :].astype(F32), store)
        act_ref[x, pl.ds(mine, chan), :] = got_ref[x, 0:chan, :]
        act_ref[x, pl.ds(rest, chan), :] = other_ref[x]
        part = lax.dot_general(act_ref[x], wide_ref[x], NT, preferred_element_type=F32)
        total = part if total is None else total + part
    out_ref[...] = total.astype(BF16)
    fetch.wait()
    full_ref[...] = lax.dot_general(held_ref[...], wide_ref[x_ref[0]], TN, preferred_element_type=F32)
    for j in range(4):
        keep_ref[j] = full_ref[pl.ds(pl.multiple_of(where_ref[j] * chan, 32), chan), :]
        give_ref[j] = full_ref[pl.ds(pl.multiple_of(where_ref[4 + j] * chan, 32), chan), :]


def sum_kernel(_a, _b, _c, parts_ref, out_ref):
    total = parts_ref[0].astype(F32)
    for k in range(1, NZ):
        total = total + parts_ref[k].astype(F32)
    out_ref[...] = total.astype(BF16)


def backward_kernel(
    own_ref, a_ref, b_ref, c_ref, maps_ref, dout_ref, gain_ref, bias_ref, pick_ref, grad_ref, sums_ref
):
    gain = column(gain_ref[...])
    dact = own_ref[...] + a_ref[...] + b_ref[...] + c_ref[...]
    normed, inverse = normalise(maps_ref[...].astype(F32))
    shifted = normed * gain + column(bias_ref[...])
    gate = jax.nn.sigmoid(shifted)
    dshift = dact * gate * (1.0 + shifted * (1.0 - gate))
    ones = jnp.ones((8, dshift.shape[1]), F32)
    exact = lax.Precision.HIGHEST
    sums_ref[0:8, :] = lax.dot_general(ones, dshift * normed, NT, precision=exact, preferred_element_type=F32)
    sums_ref[8:16, :] = lax.dot_general(ones, dshift, NT, precision=exact, preferred_element_type=F32)
    dnormed = dshift * gain
    dmaps = inverse * (dnormed - group_mean(dnormed) - normed * group_mean(dnormed * normed))
    grad_ref[...] = to_rows(dout_ref[...].astype(F32) + dmaps, pick_ref[...]).astype(BF16)


def finish_kernel(scale, x_ref, *refs):
    halves, (out_ref, tail_ref) = refs[:-2], refs[-2:]

    for k in range(NX):
        piece = jnp.concatenate([halves[2 * k][...].astype(F32), halves[2 * k + 1][...].astype(F32)], axis=0)
        out_ref[:, pl.ds(pl.multiple_of(x_ref[k] * 256, 256), 256)] = piece[0:256].T * scale
        tail_ref[pl.ds(pl.multiple_of(x_ref[k] * 64, 64), 64), :] = piece[256:320]
    out_ref[:, 1024:1280] = tail_ref[...].T * scale


def per_device(
    latents, bucket_ids, timesteps, time_table, norm_gain, norm_bias, conv_weight, cotangent
):
    dp_count = lax.axis_size("dp")
    samples, height, _, packed = latents.shape
    chan = packed // SIDE
    slots = cotangent.shape[0]
    cap = slots // dp_count
    cells = height * packed
    lanes = samples * CELLS
    wide = 9 * chan
    piece = C // NX // NZ
    scale = 1.0 / math.sqrt(samples * dp_count * CELLS)
    place = lax.axis_index("dp")
    x = place // NZ
    mine_chan = lax.axis_index("chan")
    y, core = mine_chan // 2, mine_chan % 2
    vmem = pl.BlockSpec(memory_space=pltpu.VMEM)
    smem = pl.BlockSpec(memory_space=pltpu.SMEM)
    anywhere = pl.BlockSpec(memory_space=pl.ANY)

    def move(value, dx, dz):
        pairs = [
            (i * NZ + j, (i + dx) % NX * NZ + (j + dz) % NZ) for i in range(NX) for j in range(NZ)
        ]
        return lax.ppermute(value, "dp", pairs)

    def move_chan(value, dy, flip):
        pairs = [(i * 2 + j, (i + dy) % 4 * 2 + (j ^ flip)) for i in range(4) for j in range(2)]
        return lax.ppermute(value, "chan", pairs)

    def kernel(body, out_shape, scalars, operands, name, scratch=(), vmem_mib=12, after=None, space=anywhere):
        specs = [smem] * len(scalars) + [vmem] * len(operands)
        operands = list(operands)
        if after is not None:
            at, *extra = after
            specs[len(scalars) + at : len(scalars) + at] = [space] * len(extra)
            operands[at:at] = extra
        return pl.pallas_call(
            body,
            in_specs=specs,
            out_shape=out_shape,
            scratch_shapes=list(scratch),
            name=name,
            compiler_params=pltpu.CompilerParams(vmem_limit_bytes=vmem_mib * 1024 * 1024),
            cost_estimate=pl.CostEstimate(flops=1000, bytes_accessed=1000, transcendentals=0),
        )(*scalars, *operands)

    def shape(*dims, dtype=BF16):
        return jax.ShapeDtypeStruct(dims, dtype)

    steps_y = jnp.array([0, 1, 3, 2], jnp.int32)
    to_y = (y + steps_y) % 4 * 2
    from_y = (y - steps_y) % 4 * 2
    give_where = jnp.concatenate([to_y + core, to_y + 1 - core])
    act_where = jnp.concatenate([from_y + core, from_y + 1 - core])
    core_at = core.reshape(1)
    along_z = [[j + NZ * i for j in range(NZ)] for i in range(NX)]
    along_x = [[j + NZ * i for i in range(NX)] for j in range(NZ)]
    x_ring = (x + jnp.array([0, -1, 1, 2], jnp.int32)) % NX

    gain = norm_gain.reshape(1, chan)
    bias = norm_bias.reshape(1, chan)
    weight = conv_weight.reshape(wide, C)

    same = (
        lax.broadcasted_iota(jnp.int32, (samples, 128), 0)
        == lax.broadcasted_iota(jnp.int32, (samples, 128), 1) % samples
    ).astype(BF16)
    maps, act = kernel(
        forward_kernel,
        (shape(chan, lanes), shape(chan, lanes)),
        (),
        (latents.reshape(samples, cells), same, gain, bias),
        "norm_forward",
    )
    near = [move_chan(act, 1, 0), move_chan(act, -1, 0), move_chan(act, 2, 0)]
    other = move_chan(jnp.stack([act] + near), 0, 1)
    buckets = bucket_ids[:, 0]
    order = jnp.arange(samples, dtype=jnp.int32)
    earlier = (buckets[:, None] == buckets[None, :]) & (order[None, :] < order[:, None])
    target = buckets * cap + jnp.sum(earlier.astype(jnp.int32), axis=1)
    target = jnp.tile(target, 128 // samples)
    pick = (target[None, :] == jnp.arange(slots, dtype=jnp.int32)[:, None]).astype(BF16)

    steps = jnp.tile(timesteps, 128 // samples).reshape(1, 128)
    act_half, act_all = kernel(
        place_act_kernel,
        (shape(NX, C // NX // 2, lanes), shape(C, lanes)),
        (act_where, core_at),
        (act, *near, other),
        "place_act",
    )
    got = lax.all_to_all(cotangent, "dp", split_axis=0, concat_axis=0, tiled=True)
    dout, send = kernel(
        pick_kernel,
        (shape(chan, lanes), shape(NX, 2 * chan, lanes)),
        (),
        (got.reshape(slots, cells), pick, act_half),
        "pick_dout",
    )
    got_x = lax.all_to_all(
        send, "dp", split_axis=0, concat_axis=0, tiled=True, axis_index_groups=along_x
    )
    act_other = move_chan(got_x[:, :chan], 0, 1)
    part, keep, give = kernel(
        grad_kernel,
        (shape(C // NX, wide),) + (shape(4, chan, lanes, dtype=F32),) * 2,
        (give_where, core_at, x.reshape(1)),
        (got_x, act_other),
        "grad_weight",
        scratch=[
            pltpu.VMEM((wide, C), BF16),
            pltpu.VMEM((NX, C // NX, lanes), BF16),
            pltpu.VMEM((NX, wide, lanes), BF16),
            pltpu.VMEM((C, lanes), F32),
            pltpu.SemaphoreType.DMA,
        ],
        vmem_mib=36,
        after=(2, weight),
        space=pl.BlockSpec(memory_space=pltpu.HBM),
    )
    parts = lax.all_to_all(
        part.reshape(NZ, piece, wide),
        "dp",
        split_axis=0,
        concat_axis=0,
        tiled=True,
        axis_index_groups=along_z,
    )
    sums = kernel(
        add_kernel,
        (shape(chan, lanes, dtype=F32),) * 4,
        (),
        (keep, move_chan(give, 0, 1)),
        "add_cores",
    )
    dacts = [sums[0], move_chan(sums[1], 1, 0), move_chan(sums[2], -1, 0), move_chan(sums[3], 2, 0)]
    out_rows = kernel(
        forward_conv_kernel,
        shape(slots, cells),
        (),
        (act_all, weight, maps, time_table.reshape(-1, packed), steps, pick),
        "forward_conv",
        vmem_mib=24,
        after=(6, sums[0]),
    )
    mine = kernel(sum_kernel, shape(piece, wide), (), (parts,), "sum_z", after=(0, *dacts[1:]))
    block = lax.all_gather(mine, "dp", axis=0, tiled=True, axis_index_groups=along_z)
    grad_rows, stats = kernel(
        backward_kernel,
        (shape(slots, cells), shape(16, chan, dtype=F32)),
        (),
        (*dacts, maps, dout, gain, bias, pick),
        "norm_backward",
    )

    stats = stats.reshape(2, 8, chan)[:, 0].reshape(1, 2 * chan)
    upper = stats.astype(BF16)
    lower = (stats - upper.astype(F32)).astype(BF16)
    extra = jnp.concatenate([upper, lower], axis=1).reshape(1, 1, 1, packed)
    extra = jnp.broadcast_to(extra, (dp_count, 1, height, packed))
    payload = jnp.concatenate(
        [
            out_rows.reshape(dp_count, cap, height, packed),
            grad_rows.reshape(dp_count, cap, height, packed),
            extra,
        ],
        axis=1,
    )
    payload, block = lax.optimization_barrier((payload, block))
    half = C // NX // 2
    low, high = block[:half], block[half:]
    left_low, right_high = move(low, 1, 0), move(high, -1, 0)
    left_high, right_low = move(high, 1, 0), move(low, -1, 0)
    far_low, far_high = move(left_low, 1, 0), move(right_high, -1, 0)

    back = lax.all_to_all(payload, "dp", split_axis=0, concat_axis=0, tiled=True)
    out_slots = back[:, :cap].reshape(slots, height, 1, packed)
    grad_slots = back[:, cap : 2 * cap].reshape(slots, height, 1, packed)
    sent = jnp.sum(back[:, 2 * cap, 0, :].astype(F32), axis=0)
    grad_norm = (sent[: 2 * chan] + sent[2 * chan :]).reshape(2, chan) * scale

    width = 256
    halves = (low, high, left_low, left_high, right_low, right_high, far_low, far_high)
    grad_weight = pl.pallas_call(
        functools.partial(finish_kernel, scale),
        grid=(pl.cdiv(wide, width),),
        in_specs=[smem] + [pl.BlockSpec((half, width), lambda i: (0, i))] * len(halves),
        out_specs=pl.BlockSpec((width, C), lambda i: (i, 0)),
        out_shape=jax.ShapeDtypeStruct((wide, C), F32),
        scratch_shapes=[pltpu.VMEM((256, width), F32)],
        name="grad_weight_out",
        compiler_params=pltpu.CompilerParams(vmem_limit_bytes=40 * 1024 * 1024),
    )(x_ring, *halves)
    return (out_slots, grad_slots, grad_weight.reshape(3, 3, chan, C), grad_norm)


def solution(mesh):
    in_specs = (
        P("dp", None, "chan", None),
        P("dp", None),
        P("dp"),
        P(None, "chan", None),
        P("chan"),
        P("chan"),
        P(None, None, "chan", None),
        P("dp", None, "chan", None),
    )
    out_specs = (
        P("dp", None, "chan", None),
        P("dp", None, "chan", None),
        P(None, None, "chan", None),
        P(None, "chan"),
    )
    return jax.shard_map(
        per_device, mesh=mesh, in_specs=in_specs, out_specs=out_specs, check_vma=False
    )
```

```python
import functools
import math

import jax
import jax.numpy as jnp
from jax import lax
from jax.experimental import pallas as pl
from jax.experimental.pallas import tpu as pltpu
from jax.sharding import PartitionSpec as P

C = 1280
GROUPS = 32
SIDE = 4
CELLS = 16
EPS = 1e-05
NX = 4
NZ = 8
F32 = jnp.float32
BF16 = jnp.bfloat16
NT = (((1,), (1,)), ((), ()))
TN = (((0,), (0,)), ((), ()))


def lane_block(shape):
    return (lax.broadcasted_iota(jnp.int32, shape, 1) // 32) % SIDE


def to_columns(rows, pick, chan):
    wide = lax.dot_general(rows, pick, TN, preferred_element_type=F32)
    block = lane_block((chan, 128))
    parts = []
    for h in range(SIDE):
        got = jnp.zeros((chan, 128), F32)
        for w in range(SIDE):
            start = (h * SIDE + w) * chan
            got = jnp.where(block == w, wide[start : start + chan, :], got)
        parts.append(got)
    return jnp.concatenate(parts, axis=1)


def to_rows(columns, pick):
    chan = columns.shape[0]
    block = lane_block((chan, 128))
    parts = []
    for h in range(SIDE):
        here = columns[:, 128 * h : 128 * h + 128]
        masked = [jnp.where(block == w, here, 0.0) for w in range(SIDE)]
        stack = jnp.concatenate(masked, axis=0).astype(BF16)
        parts.append(lax.dot_general(pick, stack, NT, preferred_element_type=F32))
    return jnp.concatenate(parts, axis=1)


def group_mean(values):
    chan, lanes = values.shape
    size = C // GROUPS
    spread = []
    for g in range(chan // size):
        total = jnp.sum(values[g * size : (g + 1) * size, :], axis=0, keepdims=True)
        folded = total[:, 0:128] + total[:, 128:256] + total[:, 256:384] + total[:, 384:512]
        folded = jnp.broadcast_to(folded, (8, 128))
        folded = folded + pltpu.roll(folded, 64, 1)
        folded = folded + pltpu.roll(folded, 32, 1)
        mean = folded[0:1, :] * (1.0 / (size * CELLS))
        wide = jnp.concatenate([mean] * SIDE, axis=1)
        spread.append(jnp.broadcast_to(wide, (size, lanes)))
    return jnp.concatenate(spread, axis=0)


def normalise(values):
    center = values - group_mean(values)
    inverse = lax.rsqrt(group_mean(center * center) + EPS)
    return center * inverse, inverse


def shift_rows(values, step):
    zero = jnp.zeros((values.shape[0], 128), values.dtype)
    if step == 0:
        return values
    if step > 0:
        return jnp.concatenate([values[:, 128:], zero], axis=1)
    return jnp.concatenate([zero, values[:, :-128]], axis=1)


def shift_columns(values, step):
    if step == 0:
        return values
    lanes = values.shape[1]
    block = lane_block(values.shape)
    moved = pltpu.roll(values, (-32 * step) % lanes, 1)
    return jnp.where((block + step >= 0) & (block + step < SIDE), moved, 0.0)


def im2col(dout, store):
    for col in range(3):
        moved = shift_columns(dout, -(col - 1)).astype(BF16)
        for row in range(3):
            store(row * 3 + col, shift_rows(moved, -(row - 1)))


def column(row):
    n = row.shape[1]
    eye = lax.broadcasted_iota(jnp.int32, (n, n), 0) == lax.broadcasted_iota(jnp.int32, (n, n), 1)
    return jnp.sum(jnp.where(eye, jnp.broadcast_to(row, (n, n)), 0.0), axis=1, keepdims=True)


def forward_kernel(rows_ref, pick_ref, gain_ref, bias_ref, maps_ref, act_ref):
    chan = act_ref.shape[0]
    maps = to_columns(rows_ref[...], pick_ref[...], chan)
    normed, _ = normalise(maps)
    shifted = normed * column(gain_ref[...]) + column(bias_ref[...])
    maps_ref[...] = maps.astype(BF16)
    act_ref[...] = (shifted * jax.nn.sigmoid(shifted)).astype(BF16)


def place_act_kernel(where_ref, core_ref, own_ref, a_ref, b_ref, c_ref, other_ref, half_ref, all_ref):
    chan = own_ref.shape[0]

    def put(block, value):
        all_ref[pl.ds(pl.multiple_of(block * chan, 32), chan), :] = value

    for j, ref in enumerate((own_ref, a_ref, b_ref, c_ref)):
        put(where_ref[j], ref[...])
        put(where_ref[4 + j], other_ref[j])
    for core in range(2):

        @pl.when(core_ref[0] == core)
        def _():
            for x in range(NX):
                if core == 0:
                    half_ref[x] = all_ref[256 * x : 256 * x + 160, :]
                else:
                    half_ref[x, 0:96, :] = all_ref[256 * x + 160 : 256 * x + 256, :]
                    half_ref[x, 96:160, :] = all_ref[1024 + 64 * x : 1088 + 64 * x, :]


def forward_conv_kernel(all_ref, weight_ref, maps_ref, table_ref, steps_ref, pick_ref, _, out_ref):
    chan = maps_ref.shape[0]
    conv = None
    for col in range(3):
        column_sum = None
        for row in range(3):
            tap = row * 3 + col
            term = jnp.dot(
                weight_ref[tap * chan : (tap + 1) * chan, :], all_ref[...], preferred_element_type=F32
            )
            term = shift_rows(term, row - 1)
            column_sum = term if column_sum is None else column_sum + term
        column_sum = shift_columns(column_sum, col - 1)
        conv = column_sum if conv is None else conv + column_sum
    rows = table_ref.shape[0]
    steps = steps_ref[...]
    hot = lax.broadcasted_iota(jnp.int32, (rows, 128), 0) == steps // SIDE
    wide = lax.dot_general(table_ref[...], hot.astype(BF16), TN, preferred_element_type=F32)
    embed = jnp.zeros((chan, 128), F32)
    for j in range(SIDE):
        embed = jnp.where(steps % SIDE == j, wide[j * chan : (j + 1) * chan, :], embed)
    embed = jnp.concatenate([embed] * SIDE, axis=1)
    out = maps_ref[...].astype(F32) + conv + embed
    out_ref[...] = to_rows(out, pick_ref[...]).astype(BF16)


def pick_kernel(rows_ref, pick_ref, half_ref, dout_ref, send_ref):
    chan = dout_ref.shape[0]
    dout = to_columns(rows_ref[...], pick_ref[...], chan).astype(BF16)
    dout_ref[...] = dout
    for x in range(NX):
        send_ref[x, 0:chan, :] = half_ref[x]
        send_ref[x, chan : 2 * chan, :] = dout


def add_kernel(keep_ref, got_ref, *out_refs):
    for j, ref in enumerate(out_refs):
        ref[...] = keep_ref[j] + got_ref[j]


def cut_kernel(got_ref, half_ref):
    half_ref[...] = got_ref[:, 0 : half_ref.shape[1], :]


def back_conv_kernel(where_ref, dout_ref, weight_ref, keep_ref, give_ref, wide_ref, full_ref):
    chan = dout_ref.shape[0]

    def store(tap, rows):
        wide_ref[tap * chan : (tap + 1) * chan, :] = rows

    im2col(dout_ref[...].astype(F32), store)
    full_ref[...] = lax.dot_general(weight_ref[...], wide_ref[...], TN, preferred_element_type=F32)
    for j in range(4):
        keep_ref[j] = full_ref[pl.ds(pl.multiple_of(where_ref[j] * chan, 32), chan), :]
        give_ref[j] = full_ref[pl.ds(pl.multiple_of(where_ref[4 + j] * chan, 32), chan), :]


def grad_kernel(core_ref, got_ref, other_ref, out_ref, act_ref, wide_ref):
    chan = other_ref.shape[1]
    mine = pl.multiple_of(core_ref[0] * chan, 32)
    rest = pl.multiple_of((1 - core_ref[0]) * chan, 32)
    total = None
    for x in range(NX):

        def store(tap, rows):
            wide_ref[x, tap * chan : (tap + 1) * chan, :] = rows

        im2col(got_ref[x, chan : 2 * chan, :].astype(F32), store)
        act_ref[x, pl.ds(mine, chan), :] = got_ref[x, 0:chan, :]
        act_ref[x, pl.ds(rest, chan), :] = other_ref[x]
        part = lax.dot_general(act_ref[x], wide_ref[x], NT, preferred_element_type=F32)
        total = part if total is None else total + part
    out_ref[...] = total.astype(BF16)


def sum_kernel(_a, _b, _c, parts_ref, out_ref):
    total = parts_ref[0].astype(F32)
    for k in range(1, NZ):
        total = total + parts_ref[k].astype(F32)
    out_ref[...] = total.astype(BF16)


def backward_kernel(
    own_ref, a_ref, b_ref, c_ref, maps_ref, dout_ref, gain_ref, bias_ref, pick_ref, grad_ref, sums_ref
):
    gain = column(gain_ref[...])
    dact = own_ref[...] + a_ref[...] + b_ref[...] + c_ref[...]
    normed, inverse = normalise(maps_ref[...].astype(F32))
    shifted = normed * gain + column(bias_ref[...])
    gate = jax.nn.sigmoid(shifted)
    dshift = dact * gate * (1.0 + shifted * (1.0 - gate))
    ones = jnp.ones((8, dshift.shape[1]), F32)
    exact = lax.Precision.HIGHEST
    sums_ref[0:8, :] = lax.dot_general(ones, dshift * normed, NT, precision=exact, preferred_element_type=F32)
    sums_ref[8:16, :] = lax.dot_general(ones, dshift, NT, precision=exact, preferred_element_type=F32)
    dnormed = dshift * gain
    dmaps = inverse * (dnormed - group_mean(dnormed) - normed * group_mean(dnormed * normed))
    grad_ref[...] = to_rows(dout_ref[...].astype(F32) + dmaps, pick_ref[...]).astype(BF16)


def finish_kernel(scale, x_ref, _a, _b, *refs):
    halves, (out_ref, tail_ref) = refs[:-2], refs[-2:]

    for k in range(NX):
        piece = jnp.concatenate([halves[2 * k][...].astype(F32), halves[2 * k + 1][...].astype(F32)], axis=0)
        out_ref[:, pl.ds(pl.multiple_of(x_ref[k] * 256, 256), 256)] = piece[0:256].T * scale
        tail_ref[pl.ds(pl.multiple_of(x_ref[k] * 64, 64), 64), :] = piece[256:320]
    out_ref[:, 1024:1280] = tail_ref[...].T * scale


def per_device(
    latents, bucket_ids, timesteps, time_table, norm_gain, norm_bias, conv_weight, cotangent
):
    dp_count = lax.axis_size("dp")
    samples, height, _, packed = latents.shape
    chan = packed // SIDE
    slots = cotangent.shape[0]
    cap = slots // dp_count
    cells = height * packed
    lanes = samples * CELLS
    wide = 9 * chan
    piece = C // NX // NZ
    scale = 1.0 / math.sqrt(samples * dp_count * CELLS)
    place = lax.axis_index("dp")
    x = place // NZ
    mine_chan = lax.axis_index("chan")
    y, core = mine_chan // 2, mine_chan % 2
    vmem = pl.BlockSpec(memory_space=pltpu.VMEM)
    smem = pl.BlockSpec(memory_space=pltpu.SMEM)
    anywhere = pl.BlockSpec(memory_space=pl.ANY)

    def move(value, dx, dz):
        pairs = [
            (i * NZ + j, (i + dx) % NX * NZ + (j + dz) % NZ) for i in range(NX) for j in range(NZ)
        ]
        return lax.ppermute(value, "dp", pairs)

    def move_chan(value, dy, flip):
        pairs = [(i * 2 + j, (i + dy) % 4 * 2 + (j ^ flip)) for i in range(4) for j in range(2)]
        return lax.ppermute(value, "chan", pairs)

    def kernel(body, out_shape, scalars, operands, name, scratch=(), vmem_mib=12, after=None, space=anywhere):
        specs = [smem] * len(scalars) + [vmem] * len(operands)
        operands = list(operands)
        if after is not None:
            at, *extra = after
            specs[len(scalars) + at : len(scalars) + at] = [space] * len(extra)
            operands[at:at] = extra
        return pl.pallas_call(
            body,
            in_specs=specs,
            out_shape=out_shape,
            scratch_shapes=list(scratch),
            name=name,
            compiler_params=pltpu.CompilerParams(vmem_limit_bytes=vmem_mib * 1024 * 1024),
            cost_estimate=pl.CostEstimate(flops=1000, bytes_accessed=1000, transcendentals=0),
        )(*scalars, *operands)

    def shape(*dims, dtype=BF16):
        return jax.ShapeDtypeStruct(dims, dtype)

    steps_y = jnp.array([0, 1, 3, 2], jnp.int32)
    to_y = (y + steps_y) % 4 * 2
    from_y = (y - steps_y) % 4 * 2
    give_where = jnp.concatenate([to_y + core, to_y + 1 - core])
    act_where = jnp.concatenate([from_y + core, from_y + 1 - core])
    core_at = core.reshape(1)
    along_z = [[j + NZ * i for j in range(NZ)] for i in range(NX)]
    along_x = [[j + NZ * i for i in range(NX)] for j in range(NZ)]
    x_ring = (x + jnp.array([0, -1, 1, 2], jnp.int32)) % NX

    gain = norm_gain.reshape(1, chan)
    bias = norm_bias.reshape(1, chan)
    weight = conv_weight.reshape(wide, C)

    same = (
        lax.broadcasted_iota(jnp.int32, (samples, 128), 0)
        == lax.broadcasted_iota(jnp.int32, (samples, 128), 1) % samples
    ).astype(BF16)
    maps, act = kernel(
        forward_kernel,
        (shape(chan, lanes), shape(chan, lanes)),
        (),
        (latents.reshape(samples, cells), same, gain, bias),
        "norm_forward",
    )
    near = [move_chan(act, 1, 0), move_chan(act, -1, 0), move_chan(act, 2, 0)]
    other = move_chan(jnp.stack([act] + near), 0, 1)
    buckets = bucket_ids[:, 0]
    order = jnp.arange(samples, dtype=jnp.int32)
    earlier = (buckets[:, None] == buckets[None, :]) & (order[None, :] < order[:, None])
    target = buckets * cap + jnp.sum(earlier.astype(jnp.int32), axis=1)
    target = jnp.tile(target, 128 // samples)
    pick = (target[None, :] == jnp.arange(slots, dtype=jnp.int32)[:, None]).astype(BF16)

    steps = jnp.tile(timesteps, 128 // samples).reshape(1, 128)
    act_half, act_all = kernel(
        place_act_kernel,
        (shape(NX, C // NX // 2, lanes), shape(C, lanes)),
        (act_where, core_at),
        (act, *near, other),
        "place_act",
    )
    got = lax.all_to_all(cotangent, "dp", split_axis=0, concat_axis=0, tiled=True)
    dout, send = kernel(
        pick_kernel,
        (shape(chan, lanes), shape(NX, 2 * chan, lanes)),
        (),
        (got.reshape(slots, cells), pick, act_half),
        "pick_dout",
    )
    got_x = lax.all_to_all(
        send, "dp", split_axis=0, concat_axis=0, tiled=True, axis_index_groups=along_x
    )
    keep, give = kernel(
        back_conv_kernel,
        (shape(4, chan, lanes, dtype=F32),) * 2,
        (give_where,),
        (dout, weight),
        "back_conv",
        scratch=[pltpu.VMEM((wide, lanes), BF16), pltpu.VMEM((C, lanes), F32)],
        vmem_mib=20,
    )
    act_near = kernel(cut_kernel, shape(NX, chan, lanes), (), (got_x,), "cut")
    act_other = move_chan(act_near, 0, 1)
    part = kernel(
        grad_kernel,
        shape(C // NX, wide),
        (core_at,),
        (got_x, act_other),
        "grad_weight",
        scratch=[pltpu.VMEM((NX, C // NX, lanes), BF16), pltpu.VMEM((NX, wide, lanes), BF16)],
        vmem_mib=24,
    )
    parts = lax.all_to_all(
        part.reshape(NZ, piece, wide),
        "dp",
        split_axis=0,
        concat_axis=0,
        tiled=True,
        axis_index_groups=along_z,
    )
    sums = kernel(
        add_kernel,
        (shape(chan, lanes, dtype=F32),) * 4,
        (),
        (keep, move_chan(give, 0, 1)),
        "add_cores",
    )
    dacts = [sums[0], move_chan(sums[1], 1, 0), move_chan(sums[2], -1, 0), move_chan(sums[3], 2, 0)]
    out_rows = kernel(
        forward_conv_kernel,
        shape(slots, cells),
        (),
        (act_all, weight, maps, time_table.reshape(-1, packed), steps, pick),
        "forward_conv",
        vmem_mib=24,
        after=(6, sums[0]),
    )
    mine = kernel(sum_kernel, shape(piece, wide), (), (parts,), "sum_z", after=(0, *dacts[1:]))
    block = lax.all_gather(mine, "dp", axis=0, tiled=True, axis_index_groups=along_z)
    grad_rows, stats = kernel(
        backward_kernel,
        (shape(slots, cells), shape(16, chan, dtype=F32)),
        (),
        (*dacts, maps, dout, gain, bias, pick),
        "norm_backward",
    )

    stats = stats.reshape(2, 8, chan)[:, 0].reshape(1, 2 * chan)
    upper = stats.astype(BF16)
    lower = (stats - upper.astype(F32)).astype(BF16)
    extra = jnp.concatenate([upper, lower], axis=1).reshape(1, 1, 1, packed)
    extra = jnp.broadcast_to(extra, (dp_count, 1, height, packed))
    payload = jnp.concatenate(
        [
            out_rows.reshape(dp_count, cap, height, packed),
            grad_rows.reshape(dp_count, cap, height, packed),
            extra,
        ],
        axis=1,
    )
    payload, block = lax.optimization_barrier((payload, block))
    half = C // NX // 2
    low, high = block[:half], block[half:]
    left_low, right_high = move(low, 1, 0), move(high, -1, 0)
    left_high, right_low = move(high, 1, 0), move(low, -1, 0)
    far_low, far_high = move(left_low, 1, 0), move(right_high, -1, 0)

    back = lax.all_to_all(payload, "dp", split_axis=0, concat_axis=0, tiled=True)
    out_back = back[:, :cap]
    out_slots = out_back.reshape(slots, height, 1, packed)
    grad_slots = back[:, cap : 2 * cap].reshape(slots, height, 1, packed)
    sent = jnp.sum(back[:, 2 * cap, 0, :].astype(F32), axis=0)
    grad_norm = (sent[: 2 * chan] + sent[2 * chan :]).reshape(2, chan) * scale

    width = 256
    halves = (low, high, left_low, left_high, right_low, right_high, far_low, far_high)
    grad_weight = pl.pallas_call(
        functools.partial(finish_kernel, scale),
        grid=(pl.cdiv(wide, width),),
        in_specs=[smem, anywhere, anywhere] + [pl.BlockSpec((half, width), lambda i: (0, i))] * len(halves),
        out_specs=pl.BlockSpec((width, C), lambda i: (i, 0)),
        out_shape=jax.ShapeDtypeStruct((wide, C), F32),
        scratch_shapes=[pltpu.VMEM((256, width), F32)],
        name="grad_weight_out",
        compiler_params=pltpu.CompilerParams(vmem_limit_bytes=40 * 1024 * 1024),
    )(x_ring, out_back, grad_norm, *halves)
    return (out_slots, grad_slots, grad_weight.reshape(3, 3, chan, C), grad_norm)


def solution(mesh):
    in_specs = (
        P("dp", None, "chan", None),
        P("dp", None),
        P("dp"),
        P(None, "chan", None),
        P("chan"),
        P("chan"),
        P(None, None, "chan", None),
        P("dp", None, "chan", None),
    )
    out_specs = (
        P("dp", None, "chan", None),
        P("dp", None, "chan", None),
        P(None, None, "chan", None),
        P(None, "chan"),
    )
    return jax.shard_map(
        per_device, mesh=mesh, in_specs=in_specs, out_specs=out_specs, check_vma=False
    )
```

```python
import functools
import math

import jax
import jax.numpy as jnp
from jax import lax
from jax.experimental import pallas as pl
from jax.experimental.pallas import tpu as pltpu
from jax.sharding import PartitionSpec as P

C = 1280
GROUPS = 32
SIDE = 4
CELLS = 16
EPS = 1e-05
NX = 4
NZ = 8
F32 = jnp.float32
BF16 = jnp.bfloat16
NT = (((1,), (1,)), ((), ()))
TN = (((0,), (0,)), ((), ()))


def lane_block(shape):
    return (lax.broadcasted_iota(jnp.int32, shape, 1) // 32) % SIDE


def to_columns(rows, pick, chan):
    wide = lax.dot_general(rows, pick, TN, preferred_element_type=F32)
    block = lane_block((chan, 128))
    parts = []
    for h in range(SIDE):
        got = jnp.zeros((chan, 128), F32)
        for w in range(SIDE):
            start = (h * SIDE + w) * chan
            got = jnp.where(block == w, wide[start : start + chan, :], got)
        parts.append(got)
    return jnp.concatenate(parts, axis=1)


def to_rows(columns, pick):
    chan = columns.shape[0]
    block = lane_block((chan, 128))
    parts = []
    for h in range(SIDE):
        here = columns[:, 128 * h : 128 * h + 128]
        masked = [jnp.where(block == w, here, 0.0) for w in range(SIDE)]
        stack = jnp.concatenate(masked, axis=0).astype(BF16)
        parts.append(lax.dot_general(pick, stack, NT, preferred_element_type=F32))
    return jnp.concatenate(parts, axis=1)


def group_mean(values):
    chan, lanes = values.shape
    size = C // GROUPS
    spread = []
    for g in range(chan // size):
        total = jnp.sum(values[g * size : (g + 1) * size, :], axis=0, keepdims=True)
        folded = total[:, 0:128] + total[:, 128:256] + total[:, 256:384] + total[:, 384:512]
        folded = jnp.broadcast_to(folded, (8, 128))
        folded = folded + pltpu.roll(folded, 64, 1)
        folded = folded + pltpu.roll(folded, 32, 1)
        mean = folded[0:1, :] * (1.0 / (size * CELLS))
        wide = jnp.concatenate([mean] * SIDE, axis=1)
        spread.append(jnp.broadcast_to(wide, (size, lanes)))
    return jnp.concatenate(spread, axis=0)


def normalise(values):
    center = values - group_mean(values)
    inverse = lax.rsqrt(group_mean(center * center) + EPS)
    return center * inverse, inverse


def shift_rows(values, step):
    zero = jnp.zeros((values.shape[0], 128), values.dtype)
    if step == 0:
        return values
    if step > 0:
        return jnp.concatenate([values[:, 128:], zero], axis=1)
    return jnp.concatenate([zero, values[:, :-128]], axis=1)


def shift_columns(values, step):
    if step == 0:
        return values
    lanes = values.shape[1]
    block = lane_block(values.shape)
    moved = pltpu.roll(values, (-32 * step) % lanes, 1)
    return jnp.where((block + step >= 0) & (block + step < SIDE), moved, 0.0)


def im2col(dout, store):
    for col in range(3):
        moved = shift_columns(dout, -(col - 1)).astype(BF16)
        for row in range(3):
            store(row * 3 + col, shift_rows(moved, -(row - 1)))


def column(row):
    n = row.shape[1]
    eye = lax.broadcasted_iota(jnp.int32, (n, n), 0) == lax.broadcasted_iota(jnp.int32, (n, n), 1)
    return jnp.sum(jnp.where(eye, jnp.broadcast_to(row, (n, n)), 0.0), axis=1, keepdims=True)


def forward_kernel(rows_ref, pick_ref, gain_ref, bias_ref, maps_ref, act_ref):
    chan = act_ref.shape[0]
    maps = to_columns(rows_ref[...], pick_ref[...], chan)
    normed, _ = normalise(maps)
    shifted = normed * column(gain_ref[...]) + column(bias_ref[...])
    maps_ref[...] = maps.astype(BF16)
    act_ref[...] = (shifted * jax.nn.sigmoid(shifted)).astype(BF16)


def place_act_kernel(where_ref, core_ref, own_ref, a_ref, b_ref, c_ref, other_ref, half_ref, all_ref):
    chan = own_ref.shape[0]

    def put(block, value):
        all_ref[pl.ds(pl.multiple_of(block * chan, 32), chan), :] = value

    for j, ref in enumerate((own_ref, a_ref, b_ref, c_ref)):
        put(where_ref[j], ref[...])
        put(where_ref[4 + j], other_ref[j])
    for core in range(2):

        @pl.when(core_ref[0] == core)
        def _():
            for x in range(NX):
                if core == 0:
                    half_ref[x] = all_ref[256 * x : 256 * x + 160, :]
                else:
                    half_ref[x, 0:96, :] = all_ref[256 * x + 160 : 256 * x + 256, :]
                    half_ref[x, 96:160, :] = all_ref[1024 + 64 * x : 1088 + 64 * x, :]


def forward_conv_kernel(all_ref, weight_ref, maps_ref, table_ref, steps_ref, pick_ref, _, out_ref):
    chan = maps_ref.shape[0]
    conv = None
    for col in range(3):
        column_sum = None
        for row in range(3):
            tap = row * 3 + col
            term = jnp.dot(
                weight_ref[tap * chan : (tap + 1) * chan, :], all_ref[...], preferred_element_type=F32
            )
            term = shift_rows(term, row - 1)
            column_sum = term if column_sum is None else column_sum + term
        column_sum = shift_columns(column_sum, col - 1)
        conv = column_sum if conv is None else conv + column_sum
    rows = table_ref.shape[0]
    steps = steps_ref[...]
    hot = lax.broadcasted_iota(jnp.int32, (rows, 128), 0) == steps // SIDE
    wide = lax.dot_general(table_ref[...], hot.astype(BF16), TN, preferred_element_type=F32)
    embed = jnp.zeros((chan, 128), F32)
    for j in range(SIDE):
        embed = jnp.where(steps % SIDE == j, wide[j * chan : (j + 1) * chan, :], embed)
    embed = jnp.concatenate([embed] * SIDE, axis=1)
    out = maps_ref[...].astype(F32) + conv + embed
    out_ref[...] = to_rows(out, pick_ref[...]).astype(BF16)


def pick_kernel(rows_ref, pick_ref, half_ref, dout_ref, send_ref):
    chan = dout_ref.shape[0]
    dout = to_columns(rows_ref[...], pick_ref[...], chan).astype(BF16)
    dout_ref[...] = dout
    for x in range(NX):
        send_ref[x, 0:chan, :] = half_ref[x]
        send_ref[x, chan : 2 * chan, :] = dout


def add_kernel(keep_ref, got_ref, *out_refs):
    for j, ref in enumerate(out_refs):
        ref[...] = keep_ref[j] + got_ref[j]


def cut_kernel(got_ref, half_ref):
    half_ref[...] = got_ref[:, 0 : half_ref.shape[1], :]


def back_conv_kernel(where_ref, dout_ref, weight_ref, keep_ref, give_ref, wide_ref, full_ref):
    chan = dout_ref.shape[0]

    def store(tap, rows):
        wide_ref[tap * chan : (tap + 1) * chan, :] = rows

    im2col(dout_ref[...].astype(F32), store)
    full_ref[...] = lax.dot_general(weight_ref[...], wide_ref[...], TN, preferred_element_type=F32)
    for j in range(4):
        keep_ref[j] = full_ref[pl.ds(pl.multiple_of(where_ref[j] * chan, 32), chan), :]
        give_ref[j] = full_ref[pl.ds(pl.multiple_of(where_ref[4 + j] * chan, 32), chan), :]


def grad_kernel(core_ref, got_ref, other_ref, out_ref, act_ref, wide_ref):
    chan = other_ref.shape[1]
    mine = pl.multiple_of(core_ref[0] * chan, 32)
    rest = pl.multiple_of((1 - core_ref[0]) * chan, 32)
    total = None
    for x in range(NX):

        def store(tap, rows):
            wide_ref[x, tap * chan : (tap + 1) * chan, :] = rows

        im2col(got_ref[x, chan : 2 * chan, :].astype(F32), store)
        act_ref[x, pl.ds(mine, chan), :] = got_ref[x, 0:chan, :]
        act_ref[x, pl.ds(rest, chan), :] = other_ref[x]
        part = lax.dot_general(act_ref[x], wide_ref[x], NT, preferred_element_type=F32)
        total = part if total is None else total + part
    out_ref[...] = total.astype(BF16)


def sum_kernel(_a, _b, _c, parts_ref, out_ref):
    total = parts_ref[0].astype(F32)
    for k in range(1, NZ):
        total = total + parts_ref[k].astype(F32)
    out_ref[...] = total.astype(BF16)


def backward_kernel(
    own_ref, a_ref, b_ref, c_ref, maps_ref, dout_ref, gain_ref, bias_ref, pick_ref, grad_ref, sums_ref
):
    gain = column(gain_ref[...])
    dact = own_ref[...] + a_ref[...] + b_ref[...] + c_ref[...]
    normed, inverse = normalise(maps_ref[...].astype(F32))
    shifted = normed * gain + column(bias_ref[...])
    gate = jax.nn.sigmoid(shifted)
    dshift = dact * gate * (1.0 + shifted * (1.0 - gate))
    ones = jnp.ones((8, dshift.shape[1]), F32)
    exact = lax.Precision.HIGHEST
    sums_ref[0:8, :] = lax.dot_general(ones, dshift * normed, NT, precision=exact, preferred_element_type=F32)
    sums_ref[8:16, :] = lax.dot_general(ones, dshift, NT, precision=exact, preferred_element_type=F32)
    dnormed = dshift * gain
    dmaps = inverse * (dnormed - group_mean(dnormed) - normed * group_mean(dnormed * normed))
    grad_ref[...] = to_rows(dout_ref[...].astype(F32) + dmaps, pick_ref[...]).astype(BF16)


def turn(scale, low_ref, high_ref):
    piece = jnp.concatenate([low_ref[...].astype(F32), high_ref[0:96, :].astype(F32)], axis=0)
    return piece.T * scale


def near_kernel(scale, x_ref, *refs):
    out_ref = refs[-1]
    for k in range(3):
        columns = pl.ds(pl.multiple_of(x_ref[k] * 256, 256), 256)
        out_ref[:, columns] = turn(scale, refs[2 * k], refs[2 * k + 1])


def far_kernel(scale, x_ref, _a, _b, _c, far_low_ref, far_high_ref, high_ref, left_ref, right_ref, out_ref, tail_ref):
    @pl.when(pl.program_id(1) == 0)
    def _():
        out_ref[...] = turn(scale, far_low_ref, far_high_ref)

    @pl.when(pl.program_id(1) == 1)
    def _():
        for k, ref in enumerate((high_ref, left_ref, right_ref, far_high_ref)):
            tail_ref[pl.ds(pl.multiple_of(x_ref[k] * 64, 64), 64), :] = ref[96:160, :].astype(F32)
        out_ref[...] = tail_ref[...].T * scale


def per_device(
    latents, bucket_ids, timesteps, time_table, norm_gain, norm_bias, conv_weight, cotangent
):
    dp_count = lax.axis_size("dp")
    samples, height, _, packed = latents.shape
    chan = packed // SIDE
    slots = cotangent.shape[0]
    cap = slots // dp_count
    cells = height * packed
    lanes = samples * CELLS
    wide = 9 * chan
    piece = C // NX // NZ
    scale = 1.0 / math.sqrt(samples * dp_count * CELLS)
    place = lax.axis_index("dp")
    x = place // NZ
    mine_chan = lax.axis_index("chan")
    y, core = mine_chan // 2, mine_chan % 2
    vmem = pl.BlockSpec(memory_space=pltpu.VMEM)
    smem = pl.BlockSpec(memory_space=pltpu.SMEM)
    anywhere = pl.BlockSpec(memory_space=pl.ANY)

    def move(value, dx, dz):
        pairs = [
            (i * NZ + j, (i + dx) % NX * NZ + (j + dz) % NZ) for i in range(NX) for j in range(NZ)
        ]
        return lax.ppermute(value, "dp", pairs)

    def move_chan(value, dy, flip):
        pairs = [(i * 2 + j, (i + dy) % 4 * 2 + (j ^ flip)) for i in range(4) for j in range(2)]
        return lax.ppermute(value, "chan", pairs)

    def kernel(body, out_shape, scalars, operands, name, scratch=(), vmem_mib=12, after=None, space=anywhere):
        specs = [smem] * len(scalars) + [vmem] * len(operands)
        operands = list(operands)
        if after is not None:
            at, *extra = after
            specs[len(scalars) + at : len(scalars) + at] = [space] * len(extra)
            operands[at:at] = extra
        return pl.pallas_call(
            body,
            in_specs=specs,
            out_shape=out_shape,
            scratch_shapes=list(scratch),
            name=name,
            compiler_params=pltpu.CompilerParams(vmem_limit_bytes=vmem_mib * 1024 * 1024),
            cost_estimate=pl.CostEstimate(flops=1000, bytes_accessed=1000, transcendentals=0),
        )(*scalars, *operands)

    def shape(*dims, dtype=BF16):
        return jax.ShapeDtypeStruct(dims, dtype)

    steps_y = jnp.array([0, 1, 3, 2], jnp.int32)
    to_y = (y + steps_y) % 4 * 2
    from_y = (y - steps_y) % 4 * 2
    give_where = jnp.concatenate([to_y + core, to_y + 1 - core])
    act_where = jnp.concatenate([from_y + core, from_y + 1 - core])
    core_at = core.reshape(1)
    along_z = [[j + NZ * i for j in range(NZ)] for i in range(NX)]
    along_x = [[j + NZ * i for i in range(NX)] for j in range(NZ)]
    x_ring = (x + jnp.array([0, -1, 1, 2], jnp.int32)) % NX

    gain = norm_gain.reshape(1, chan)
    bias = norm_bias.reshape(1, chan)
    weight = conv_weight.reshape(wide, C)

    same = (
        lax.broadcasted_iota(jnp.int32, (samples, 128), 0)
        == lax.broadcasted_iota(jnp.int32, (samples, 128), 1) % samples
    ).astype(BF16)
    maps, act = kernel(
        forward_kernel,
        (shape(chan, lanes), shape(chan, lanes)),
        (),
        (latents.reshape(samples, cells), same, gain, bias),
        "norm_forward",
    )
    near = [move_chan(act, 1, 0), move_chan(act, -1, 0), move_chan(act, 2, 0)]
    other = move_chan(jnp.stack([act] + near), 0, 1)
    buckets = bucket_ids[:, 0]
    order = jnp.arange(samples, dtype=jnp.int32)
    earlier = (buckets[:, None] == buckets[None, :]) & (order[None, :] < order[:, None])
    target = buckets * cap + jnp.sum(earlier.astype(jnp.int32), axis=1)
    target = jnp.tile(target, 128 // samples)
    pick = (target[None, :] == jnp.arange(slots, dtype=jnp.int32)[:, None]).astype(BF16)

    steps = jnp.tile(timesteps, 128 // samples).reshape(1, 128)
    act_half, act_all = kernel(
        place_act_kernel,
        (shape(NX, C // NX // 2, lanes), shape(C, lanes)),
        (act_where, core_at),
        (act, *near, other),
        "place_act",
    )
    got = lax.all_to_all(cotangent, "dp", split_axis=0, concat_axis=0, tiled=True)
    dout, send = kernel(
        pick_kernel,
        (shape(chan, lanes), shape(NX, 2 * chan, lanes)),
        (),
        (got.reshape(slots, cells), pick, act_half),
        "pick_dout",
    )
    got_x = lax.all_to_all(
        send, "dp", split_axis=0, concat_axis=0, tiled=True, axis_index_groups=along_x
    )
    keep, give = kernel(
        back_conv_kernel,
        (shape(4, chan, lanes, dtype=F32),) * 2,
        (give_where,),
        (dout, weight),
        "back_conv",
        scratch=[pltpu.VMEM((wide, lanes), BF16), pltpu.VMEM((C, lanes), F32)],
        vmem_mib=20,
    )
    act_near = kernel(cut_kernel, shape(NX, chan, lanes), (), (got_x,), "cut")
    act_other = move_chan(act_near, 0, 1)
    part = kernel(
        grad_kernel,
        shape(C // NX, wide),
        (core_at,),
        (got_x, act_other),
        "grad_weight",
        scratch=[pltpu.VMEM((NX, C // NX, lanes), BF16), pltpu.VMEM((NX, wide, lanes), BF16)],
        vmem_mib=24,
    )
    parts = lax.all_to_all(
        part.reshape(NZ, piece, wide),
        "dp",
        split_axis=0,
        concat_axis=0,
        tiled=True,
        axis_index_groups=along_z,
    )
    sums = kernel(
        add_kernel,
        (shape(chan, lanes, dtype=F32),) * 4,
        (),
        (keep, move_chan(give, 0, 1)),
        "add_cores",
    )
    dacts = [sums[0], move_chan(sums[1], 1, 0), move_chan(sums[2], -1, 0), move_chan(sums[3], 2, 0)]
    out_rows = kernel(
        forward_conv_kernel,
        shape(slots, cells),
        (),
        (act_all, weight, maps, time_table.reshape(-1, packed), steps, pick),
        "forward_conv",
        vmem_mib=24,
        after=(6, sums[0]),
    )
    mine = kernel(sum_kernel, shape(piece, wide), (), (parts,), "sum_z", after=(0, *dacts[1:]))
    block = lax.all_gather(mine, "dp", axis=0, tiled=True, axis_index_groups=along_z)
    grad_rows, stats = kernel(
        backward_kernel,
        (shape(slots, cells), shape(16, chan, dtype=F32)),
        (),
        (*dacts, maps, dout, gain, bias, pick),
        "norm_backward",
    )

    stats = stats.reshape(2, 8, chan)[:, 0].reshape(1, 2 * chan)
    upper = stats.astype(BF16)
    lower = (stats - upper.astype(F32)).astype(BF16)
    extra = jnp.concatenate([upper, lower], axis=1).reshape(1, 1, 1, packed)
    extra = jnp.broadcast_to(extra, (dp_count, 1, height, packed))
    payload = jnp.concatenate(
        [
            out_rows.reshape(dp_count, cap, height, packed),
            grad_rows.reshape(dp_count, cap, height, packed),
            extra,
        ],
        axis=1,
    )
    payload, block = lax.optimization_barrier((payload, block))
    half = C // NX // 2
    low, high = block[:half], block[half:]
    left_low, right_high = move(low, 1, 0), move(high, -1, 0)
    left_high, right_low = move(high, 1, 0), move(low, -1, 0)
    far_low, far_high = move(left_low, 1, 0), move(right_high, -1, 0)

    back = lax.all_to_all(payload, "dp", split_axis=0, concat_axis=0, tiled=True)
    out_back = back[:, :cap]
    out_slots = out_back.reshape(slots, height, 1, packed)
    grad_slots = back[:, cap : 2 * cap].reshape(slots, height, 1, packed)
    sent = jnp.sum(back[:, 2 * cap, 0, :].astype(F32), axis=0)
    grad_norm = (sent[: 2 * chan] + sent[2 * chan :]).reshape(2, chan) * scale

    width = 256
    nearby = (low, high, left_low, left_high, right_low, right_high)
    params = pltpu.CompilerParams(vmem_limit_bytes=24 * 1024 * 1024)
    grad_weight = pl.pallas_call(
        functools.partial(near_kernel, scale),
        grid=(pl.cdiv(wide, width),),
        in_specs=[smem] + [pl.BlockSpec((half, width), lambda i: (0, i))] * len(nearby),
        out_specs=pl.BlockSpec((width, C), lambda i: (i, 0)),
        out_shape=jax.ShapeDtypeStruct((wide, C), F32),
        name="grad_weight_near",
        compiler_params=params,
    )(x_ring, *nearby)
    grad_weight = pl.pallas_call(
        functools.partial(far_kernel, scale),
        grid_spec=pltpu.PrefetchScalarGridSpec(
            num_scalar_prefetch=1,
            grid=(pl.cdiv(wide, width), 2),
            in_specs=[anywhere] * 3 + [pl.BlockSpec((half, width), lambda i, j, where: (0, i))] * 5,
            out_specs=pl.BlockSpec((width, width), lambda i, j, where: (i, jnp.where(j == 0, where[3], NX))),
            scratch_shapes=[pltpu.VMEM((width, width), F32)],
        ),
        out_shape=jax.ShapeDtypeStruct((wide, C), F32),
        input_output_aliases={1: 0},
        name="grad_weight_far",
        compiler_params=params,
    )(x_ring, grad_weight, out_back, grad_norm, far_low, far_high, high, left_high, right_high)
    return (out_slots, grad_slots, grad_weight.reshape(3, 3, chan, C), grad_norm)


def solution(mesh):
    in_specs = (
        P("dp", None, "chan", None),
        P("dp", None),
        P("dp"),
        P(None, "chan", None),
        P("chan"),
        P("chan"),
        P(None, None, "chan", None),
        P("dp", None, "chan", None),
    )
    out_specs = (
        P("dp", None, "chan", None),
        P("dp", None, "chan", None),
        P(None, None, "chan", None),
        P(None, "chan"),
    )
    return jax.shard_map(
        per_device, mesh=mesh, in_specs=in_specs, out_specs=out_specs, check_vma=False
    )
```

```python
import functools
import math

import jax
import jax.numpy as jnp
from jax import lax
from jax.experimental import pallas as pl
from jax.experimental.pallas import tpu as pltpu
from jax.sharding import PartitionSpec as P

C = 1280
GROUPS = 32
SIDE = 4
CELLS = 16
EPS = 1e-05
NX = 4
NZ = 8
F32 = jnp.float32
BF16 = jnp.bfloat16
NT = (((1,), (1,)), ((), ()))
TN = (((0,), (0,)), ((), ()))


def lane_block(shape):
    return (lax.broadcasted_iota(jnp.int32, shape, 1) // 32) % SIDE


def to_columns(rows, pick, chan):
    wide = lax.dot_general(rows, pick, TN, preferred_element_type=F32)
    block = lane_block((chan, 128))
    parts = []
    for h in range(SIDE):
        got = jnp.zeros((chan, 128), F32)
        for w in range(SIDE):
            start = (h * SIDE + w) * chan
            got = jnp.where(block == w, wide[start : start + chan, :], got)
        parts.append(got)
    return jnp.concatenate(parts, axis=1)


def to_rows(columns, pick):
    chan = columns.shape[0]
    block = lane_block((chan, 128))
    parts = []
    for h in range(SIDE):
        here = columns[:, 128 * h : 128 * h + 128]
        masked = [jnp.where(block == w, here, 0.0) for w in range(SIDE)]
        stack = jnp.concatenate(masked, axis=0).astype(BF16)
        parts.append(lax.dot_general(pick, stack, NT, preferred_element_type=F32))
    return jnp.concatenate(parts, axis=1)


def group_mean(values):
    chan, lanes = values.shape
    size = C // GROUPS
    spread = []
    for g in range(chan // size):
        total = jnp.sum(values[g * size : (g + 1) * size, :], axis=0, keepdims=True)
        folded = total[:, 0:128] + total[:, 128:256] + total[:, 256:384] + total[:, 384:512]
        folded = jnp.broadcast_to(folded, (8, 128))
        folded = folded + pltpu.roll(folded, 64, 1)
        folded = folded + pltpu.roll(folded, 32, 1)
        mean = folded[0:1, :] * (1.0 / (size * CELLS))
        wide = jnp.concatenate([mean] * SIDE, axis=1)
        spread.append(jnp.broadcast_to(wide, (size, lanes)))
    return jnp.concatenate(spread, axis=0)


def normalise(values):
    center = values - group_mean(values)
    inverse = lax.rsqrt(group_mean(center * center) + EPS)
    return center * inverse, inverse


def shift_rows(values, step):
    zero = jnp.zeros((values.shape[0], 128), values.dtype)
    if step == 0:
        return values
    if step > 0:
        return jnp.concatenate([values[:, 128:], zero], axis=1)
    return jnp.concatenate([zero, values[:, :-128]], axis=1)


def shift_columns(values, step):
    if step == 0:
        return values
    lanes = values.shape[1]
    block = lane_block(values.shape)
    moved = pltpu.roll(values, (-32 * step) % lanes, 1)
    return jnp.where((block + step >= 0) & (block + step < SIDE), moved, 0.0)


def im2col(dout, store):
    for col in range(3):
        moved = shift_columns(dout, -(col - 1)).astype(BF16)
        for row in range(3):
            store(row * 3 + col, shift_rows(moved, -(row - 1)))


def column(row):
    n = row.shape[1]
    eye = lax.broadcasted_iota(jnp.int32, (n, n), 0) == lax.broadcasted_iota(jnp.int32, (n, n), 1)
    return jnp.sum(jnp.where(eye, jnp.broadcast_to(row, (n, n)), 0.0), axis=1, keepdims=True)


def forward_kernel(rows_ref, pick_ref, affine_ref, maps_ref, act_ref):
    chan = act_ref.shape[0]
    maps = to_columns(rows_ref[...], pick_ref[...], chan)
    normed, _ = normalise(maps)
    shifted = normed * column(affine_ref[0:1, :]) + column(affine_ref[1:2, :])
    maps_ref[...] = maps.astype(BF16)
    act_ref[...] = (shifted * jax.nn.sigmoid(shifted)).astype(BF16)


def place_act_kernel(where_ref, core_ref, own_ref, a_ref, b_ref, c_ref, other_ref, half_ref, all_ref):
    chan = own_ref.shape[0]

    def put(block, value):
        all_ref[pl.ds(pl.multiple_of(block * chan, 32), chan), :] = value

    for j, ref in enumerate((own_ref, a_ref, b_ref, c_ref)):
        put(where_ref[j], ref[...])
        put(where_ref[4 + j], other_ref[j])
    for core in range(2):

        @pl.when(core_ref[0] == core)
        def _():
            for x in range(NX):
                if core == 0:
                    half_ref[x] = all_ref[256 * x : 256 * x + 160, :]
                else:
                    half_ref[x, 0:96, :] = all_ref[256 * x + 160 : 256 * x + 256, :]
                    half_ref[x, 96:160, :] = all_ref[1024 + 64 * x : 1088 + 64 * x, :]


def forward_conv_kernel(all_ref, weight_ref, maps_ref, table_ref, steps_ref, pick_ref, _, out_ref):
    chan = maps_ref.shape[0]
    conv = None
    for col in range(3):
        column_sum = None
        for row in range(3):
            tap = row * 3 + col
            term = jnp.dot(
                weight_ref[tap * chan : (tap + 1) * chan, :], all_ref[...], preferred_element_type=F32
            )
            term = shift_rows(term, row - 1)
            column_sum = term if column_sum is None else column_sum + term
        column_sum = shift_columns(column_sum, col - 1)
        conv = column_sum if conv is None else conv + column_sum
    rows = table_ref.shape[0]
    steps = steps_ref[...]
    hot = lax.broadcasted_iota(jnp.int32, (rows, 128), 0) == steps // SIDE
    wide = lax.dot_general(table_ref[...], hot.astype(BF16), TN, preferred_element_type=F32)
    embed = jnp.zeros((chan, 128), F32)
    for j in range(SIDE):
        embed = jnp.where(steps % SIDE == j, wide[j * chan : (j + 1) * chan, :], embed)
    embed = jnp.concatenate([embed] * SIDE, axis=1)
    out = maps_ref[...].astype(F32) + conv + embed
    out_ref[...] = to_rows(out, pick_ref[...]).astype(BF16)


def pick_kernel(rows_ref, pick_ref, half_ref, dout_ref, send_ref):
    chan = dout_ref.shape[0]
    dout = to_columns(rows_ref[...], pick_ref[...], chan).astype(BF16)
    dout_ref[...] = dout
    for x in range(NX):
        send_ref[x, 0:chan, :] = half_ref[x]
        send_ref[x, chan : 2 * chan, :] = dout


def add_kernel(keep_ref, got_ref, *out_refs):
    for j, ref in enumerate(out_refs):
        ref[...] = keep_ref[j] + got_ref[j]


def cut_kernel(got_ref, half_ref):
    half_ref[...] = got_ref[:, 0 : half_ref.shape[1], :]


def back_conv_kernel(where_ref, dout_ref, weight_ref, keep_ref, give_ref, wide_ref, full_ref):
    chan = dout_ref.shape[0]

    def store(tap, rows):
        wide_ref[tap * chan : (tap + 1) * chan, :] = rows

    im2col(dout_ref[...].astype(F32), store)
    full_ref[...] = lax.dot_general(weight_ref[...], wide_ref[...], TN, preferred_element_type=F32)
    for j in range(4):
        keep_ref[j] = full_ref[pl.ds(pl.multiple_of(where_ref[j] * chan, 32), chan), :]
        give_ref[j] = full_ref[pl.ds(pl.multiple_of(where_ref[4 + j] * chan, 32), chan), :]


def grad_kernel(core_ref, got_ref, other_ref, out_ref, act_ref, wide_ref):
    chan = other_ref.shape[1]
    mine = pl.multiple_of(core_ref[0] * chan, 32)
    rest = pl.multiple_of((1 - core_ref[0]) * chan, 32)
    total = None
    for x in range(NX):

        def store(tap, rows):
            wide_ref[x, tap * chan : (tap + 1) * chan, :] = rows

        im2col(got_ref[x, chan : 2 * chan, :].astype(F32), store)
        act_ref[x, pl.ds(mine, chan), :] = got_ref[x, 0:chan, :]
        act_ref[x, pl.ds(rest, chan), :] = other_ref[x]
        part = lax.dot_general(act_ref[x], wide_ref[x], NT, preferred_element_type=F32)
        total = part if total is None else total + part
    out_ref[...] = total.astype(BF16)


def sum_kernel(_a, _b, _c, parts_ref, out_ref):
    total = parts_ref[0].astype(F32)
    for k in range(1, NZ):
        total = total + parts_ref[k].astype(F32)
    out_ref[...] = total.astype(BF16)


def backward_kernel(
    own_ref, a_ref, b_ref, c_ref, maps_ref, dout_ref, affine_ref, pick_ref, grad_ref, sums_ref
):
    gain = column(affine_ref[0:1, :])
    dact = own_ref[...] + a_ref[...] + b_ref[...] + c_ref[...]
    normed, inverse = normalise(maps_ref[...].astype(F32))
    shifted = normed * gain + column(affine_ref[1:2, :])
    gate = jax.nn.sigmoid(shifted)
    dshift = dact * gate * (1.0 + shifted * (1.0 - gate))
    ones = jnp.ones((8, dshift.shape[1]), F32)
    exact = lax.Precision.HIGHEST
    sums_ref[0:8, :] = lax.dot_general(ones, dshift * normed, NT, precision=exact, preferred_element_type=F32)
    sums_ref[8:16, :] = lax.dot_general(ones, dshift, NT, precision=exact, preferred_element_type=F32)
    dnormed = dshift * gain
    dmaps = inverse * (dnormed - group_mean(dnormed) - normed * group_mean(dnormed * normed))
    grad_ref[...] = to_rows(dout_ref[...].astype(F32) + dmaps, pick_ref[...]).astype(BF16)


def finish_kernel(scale, x_ref, _a, _b, *refs):
    halves, (out_ref, tail_ref) = refs[:-2], refs[-2:]

    for k in range(NX):
        piece = jnp.concatenate([halves[2 * k][...].astype(F32), halves[2 * k + 1][...].astype(F32)], axis=0)
        out_ref[:, pl.ds(pl.multiple_of(x_ref[k] * 256, 256), 256)] = piece[0:256].T * scale
        tail_ref[pl.ds(pl.multiple_of(x_ref[k] * 64, 64), 64), :] = piece[256:320]
    out_ref[:, 1024:1280] = tail_ref[...].T * scale


def per_device(
    latents, bucket_ids, timesteps, time_table, norm_gain, norm_bias, conv_weight, cotangent
):
    dp_count = lax.axis_size("dp")
    samples, height, _, packed = latents.shape
    chan = packed // SIDE
    slots = cotangent.shape[0]
    cap = slots // dp_count
    cells = height * packed
    lanes = samples * CELLS
    wide = 9 * chan
    piece = C // NX // NZ
    scale = 1.0 / math.sqrt(samples * dp_count * CELLS)
    place = lax.axis_index("dp")
    x = place // NZ
    mine_chan = lax.axis_index("chan")
    y, core = mine_chan // 2, mine_chan % 2
    vmem = pl.BlockSpec(memory_space=pltpu.VMEM)
    smem = pl.BlockSpec(memory_space=pltpu.SMEM)
    anywhere = pl.BlockSpec(memory_space=pl.ANY)

    def move(value, dx, dz):
        pairs = [
            (i * NZ + j, (i + dx) % NX * NZ + (j + dz) % NZ) for i in range(NX) for j in range(NZ)
        ]
        return lax.ppermute(value, "dp", pairs)

    def move_chan(value, dy, flip):
        pairs = [(i * 2 + j, (i + dy) % 4 * 2 + (j ^ flip)) for i in range(4) for j in range(2)]
        return lax.ppermute(value, "chan", pairs)

    def kernel(body, out_shape, scalars, operands, name, scratch=(), vmem_mib=12, after=None, space=anywhere):
        specs = [smem] * len(scalars) + [vmem] * len(operands)
        operands = list(operands)
        if after is not None:
            at, *extra = after
            specs[len(scalars) + at : len(scalars) + at] = [space] * len(extra)
            operands[at:at] = extra
        return pl.pallas_call(
            body,
            in_specs=specs,
            out_shape=out_shape,
            scratch_shapes=list(scratch),
            name=name,
            compiler_params=pltpu.CompilerParams(vmem_limit_bytes=vmem_mib * 1024 * 1024),
            cost_estimate=pl.CostEstimate(flops=1000, bytes_accessed=1000, transcendentals=0),
        )(*scalars, *operands)

    def shape(*dims, dtype=BF16):
        return jax.ShapeDtypeStruct(dims, dtype)

    steps_y = jnp.array([0, 1, 3, 2], jnp.int32)
    to_y = (y + steps_y) % 4 * 2
    from_y = (y - steps_y) % 4 * 2
    give_where = jnp.concatenate([to_y + core, to_y + 1 - core])
    act_where = jnp.concatenate([from_y + core, from_y + 1 - core])
    core_at = core.reshape(1)
    along_z = [[j + NZ * i for j in range(NZ)] for i in range(NX)]
    along_x = [[j + NZ * i for i in range(NX)] for j in range(NZ)]
    x_ring = (x + jnp.array([0, -1, 1, 2], jnp.int32)) % NX

    affine = jnp.stack([norm_gain, norm_bias])
    weight = conv_weight.reshape(wide, C)

    same = (
        lax.broadcasted_iota(jnp.int32, (samples, 128), 0)
        == lax.broadcasted_iota(jnp.int32, (samples, 128), 1) % samples
    ).astype(BF16)
    maps, act = kernel(
        forward_kernel,
        (shape(chan, lanes), shape(chan, lanes)),
        (),
        (latents.reshape(samples, cells), same, affine),
        "norm_forward",
    )
    near = [move_chan(act, 1, 0), move_chan(act, -1, 0), move_chan(act, 2, 0)]
    other = move_chan(jnp.stack([act] + near), 0, 1)
    buckets = bucket_ids[:, 0]
    order = jnp.arange(samples, dtype=jnp.int32)
    earlier = (buckets[:, None] == buckets[None, :]) & (order[None, :] < order[:, None])
    target = buckets * cap + jnp.sum(earlier.astype(jnp.int32), axis=1)
    target = jnp.tile(target, 128 // samples)
    pick = (target[None, :] == jnp.arange(slots, dtype=jnp.int32)[:, None]).astype(BF16)

    steps = jnp.tile(timesteps, 128 // samples).reshape(1, 128)
    act_half, act_all = kernel(
        place_act_kernel,
        (shape(NX, C // NX // 2, lanes), shape(C, lanes)),
        (act_where, core_at),
        (act, *near, other),
        "place_act",
    )
    got = lax.all_to_all(cotangent, "dp", split_axis=0, concat_axis=0, tiled=True)
    dout, send = kernel(
        pick_kernel,
        (shape(chan, lanes), shape(NX, 2 * chan, lanes)),
        (),
        (got.reshape(slots, cells), pick, act_half),
        "pick_dout",
    )
    got_x = lax.all_to_all(
        send, "dp", split_axis=0, concat_axis=0, tiled=True, axis_index_groups=along_x
    )
    keep, give = kernel(
        back_conv_kernel,
        (shape(4, chan, lanes, dtype=F32),) * 2,
        (give_where,),
        (dout, weight),
        "back_conv",
        scratch=[pltpu.VMEM((wide, lanes), BF16), pltpu.VMEM((C, lanes), F32)],
        vmem_mib=20,
    )
    act_near = kernel(cut_kernel, shape(NX, chan, lanes), (), (got_x,), "cut")
    act_other = move_chan(act_near, 0, 1)
    part = kernel(
        grad_kernel,
        shape(C // NX, wide),
        (core_at,),
        (got_x, act_other),
        "grad_weight",
        scratch=[pltpu.VMEM((NX, C // NX, lanes), BF16), pltpu.VMEM((NX, wide, lanes), BF16)],
        vmem_mib=24,
    )
    parts = lax.all_to_all(
        part.reshape(NZ, piece, wide),
        "dp",
        split_axis=0,
        concat_axis=0,
        tiled=True,
        axis_index_groups=along_z,
    )
    sums = kernel(
        add_kernel,
        (shape(chan, lanes, dtype=F32),) * 4,
        (),
        (keep, move_chan(give, 0, 1)),
        "add_cores",
    )
    dacts = [sums[0], move_chan(sums[1], 1, 0), move_chan(sums[2], -1, 0), move_chan(sums[3], 2, 0)]
    out_rows = kernel(
        forward_conv_kernel,
        shape(slots, cells),
        (),
        (act_all, weight, maps, time_table.reshape(-1, packed), steps, pick),
        "forward_conv",
        vmem_mib=24,
        after=(6, sums[0]),
    )
    mine = kernel(sum_kernel, shape(piece, wide), (), (parts,), "sum_z", after=(0, *dacts[1:]))
    block = lax.all_gather(mine, "dp", axis=0, tiled=True, axis_index_groups=along_z)
    grad_rows, stats = kernel(
        backward_kernel,
        (shape(slots, cells), shape(16, chan, dtype=F32)),
        (),
        (*dacts, maps, dout, affine, pick),
        "norm_backward",
    )

    stats = stats.reshape(2, 8, chan)[:, 0].reshape(1, 2 * chan)
    upper = stats.astype(BF16)
    lower = (stats - upper.astype(F32)).astype(BF16)
    extra = jnp.concatenate([upper, lower], axis=1).reshape(1, 1, 1, packed)
    extra = jnp.broadcast_to(extra, (dp_count, 1, height, packed))
    payload = jnp.concatenate(
        [
            out_rows.reshape(dp_count, cap, height, packed),
            grad_rows.reshape(dp_count, cap, height, packed),
            extra,
        ],
        axis=1,
    )
    payload, block = lax.optimization_barrier((payload, block))
    half = C // NX // 2
    low, high = block[:half], block[half:]
    left_low, right_high = move(low, 1, 0), move(high, -1, 0)
    left_high, right_low = move(high, 1, 0), move(low, -1, 0)
    far_low, far_high = move(left_low, 1, 0), move(right_high, -1, 0)

    back = lax.all_to_all(payload, "dp", split_axis=0, concat_axis=0, tiled=True)
    out_back = back[:, :cap]
    out_slots = out_back.reshape(slots, height, 1, packed)
    grad_slots = back[:, cap : 2 * cap].reshape(slots, height, 1, packed)
    sent = jnp.sum(back[:, 2 * cap, 0, :].astype(F32), axis=0)
    grad_norm = (sent[: 2 * chan] + sent[2 * chan :]).reshape(2, chan) * scale

    width = 256
    halves = (low, high, left_low, left_high, right_low, right_high, far_low, far_high)
    grad_weight = pl.pallas_call(
        functools.partial(finish_kernel, scale),
        grid=(pl.cdiv(wide, width),),
        in_specs=[smem, anywhere, anywhere] + [pl.BlockSpec((half, width), lambda i: (0, i))] * len(halves),
        out_specs=pl.BlockSpec((width, C), lambda i: (i, 0)),
        out_shape=jax.ShapeDtypeStruct((wide, C), F32),
        scratch_shapes=[pltpu.VMEM((256, width), F32)],
        name="grad_weight_out",
        compiler_params=pltpu.CompilerParams(vmem_limit_bytes=12 * 1024 * 1024),
    )(x_ring, out_back, grad_norm, *halves)
    return (out_slots, grad_slots, grad_weight.reshape(3, 3, chan, C), grad_norm)


def solution(mesh):
    in_specs = (
        P("dp", None, "chan", None),
        P("dp", None),
        P("dp"),
        P(None, "chan", None),
        P("chan"),
        P("chan"),
        P(None, None, "chan", None),
        P("dp", None, "chan", None),
    )
    out_specs = (
        P("dp", None, "chan", None),
        P("dp", None, "chan", None),
        P(None, None, "chan", None),
        P(None, "chan"),
    )
    return jax.shard_map(
        per_device, mesh=mesh, in_specs=in_specs, out_specs=out_specs, check_vma=False
    )
```
